512 devices in a mesh: seq: 128 (over z, y, core), tensor: 4 (over x).
Axes of the slice: x: 4, y: 8, z: 8, core: 2. Of those that a mesh axis runs over, the one named last changes fastest.
Arguments:
- query: bfloat16 [128, 3072], P('seq', 'tensor'), may hold values from -6 to 6
- page_owner: int32 [2048], P('seq'), may hold values from 0 to 127, as said below
- page_fill: int32 [2048], P('seq'), may hold values from 0 to 64, as said below
- cache: bfloat16 [2048, 64, 576], P('seq'), may hold values from -32 to 32
- w_uk: bfloat16 [16, 128, 512], P('tensor'), may hold values from -0.5 to 0.5
- w_uv: bfloat16 [16, 512, 128], P('tensor'), may hold values from -0.25 to 0.25
- w_out: bfloat16 [2048, 2048], P('tensor'), may hold values from -0.125 to 0.125
Outputs:
- attn_out: bfloat16 [128, 2048], P('seq', 'tensor')
The draws below stay inside these ranges and needn't reach their ends.
Inputs may be any that keep to these rules, and one draw needn't show every extreme that they name: `page_owner`: slots with page_fill 0 are unused and name request 0; every request has at least one page with page_fill 1 or more; a device's used slots come first among its 16; some device uses all 16. `page_fill`: the first slot of every device is full.
All inputs are finite; a program needn't handle non-finite values.
Results may differ from the reference program's by a relative error of at most 0.014.
Values may be sent and summed in bfloat16 or wider, within the bound.
A program may use at most 64 MiB of HBM per device.

```python
import math
import jax
import jax.numpy as jnp
from jax import lax

D = 2048
H = 16
NOPE = 128
ROPE = 64
LATENT = 512
VDIM = 128
PAGE = 64
RQ_DEV = 1
PAGES_DEV = 16
REQUESTS = 128
PAGES = 2048


def page_layout(key):
    devices = PAGES // PAGES_DEV
    lowest = max(RQ_DEV, PAGES_DEV // 4)
    live = jax.random.randint(jax.random.fold_in(key, 101), (devices,), lowest, PAGES_DEV + 1)
    full_device = jax.random.randint(jax.random.fold_in(key, 102), (), 0, devices)
    live = jnp.where(jnp.arange(devices) == full_device, PAGES_DEV, live)
    slot = jnp.arange(PAGES) % PAGES_DEV
    device = jnp.arange(PAGES) // PAGES_DEV
    alive = slot < live[device]
    ranks = jnp.cumsum(alive.astype(jnp.int32)) - 1
    heavy = jax.random.randint(jax.random.fold_in(key, 103), (), 0, REQUESTS)
    picked = jax.random.randint(jax.random.fold_in(key, 104), (PAGES,), 0, REQUESTS)
    coin = jax.random.randint(jax.random.fold_in(key, 105), (PAGES,), 0, 2)
    others = jnp.where(coin == 0, heavy, picked)
    shuffle = jax.random.permutation(jax.random.fold_in(key, 106), REQUESTS)
    first = jnp.take(shuffle, jnp.clip(ranks, 0, REQUESTS - 1))
    owner = jnp.where(ranks < REQUESTS, first, others)
    owner = jnp.where(alive, owner, 0).astype(jnp.int32)
    fill = jax.random.randint(jax.random.fold_in(key, 107), (PAGES,), 1, PAGE + 1)
    fill = jnp.where(slot == 0, PAGE, fill)
    fill = jnp.where(alive, fill, 0).astype(jnp.int32)
    return (owner, fill)


def query_values(key):
    shape = (REQUESTS, H * (NOPE + ROPE))
    base = jnp.clip(jax.random.normal(jax.random.fold_in(key, 201), shape, jnp.float32), -4.0, 4.0)
    return base


def draw_query(key, part):
    base = query_values(key)
    return base.astype(jnp.bfloat16)


def draw_page_owner(key, part):
    owner, fill = page_layout(key)
    return owner


def draw_page_fill(key, part):
    owner, fill = page_layout(key)
    return fill


def draw_cache(key, part):
    shape = (PAGES, PAGE, LATENT + ROPE)
    values = jnp.clip(jax.random.normal(jax.random.fold_in(key, 301), shape, jnp.float32), -4.0, 4.0)
    return values.astype(jnp.bfloat16)


def shard_levels(own_key, extent, pieces, low, high):
    def one(axis_at, shards_of):
        heights = jax.random.uniform(jax.random.fold_in(jax.random.fold_in(own_key, 6), axis_at), (shards_of,), jnp.float32, low / len(pieces), high / len(pieces))
        return jnp.repeat(jnp.exp(heights), extent[axis_at] // shards_of).reshape((-1,) + (1,) * (len(extent) - axis_at - 1))

    gain = one(*pieces[0])
    for cut in pieces[1:]:
        gain = gain * one(*cut)
    return gain


def scatter_about(rng, shape, width, bound, pieces=(), held_as=jnp.bfloat16):
    values = jax.random.normal(rng, shape, jnp.float32) * width
    if len(pieces) > 0:
        values = shard_levels(rng, shape, pieces, -0.22, 0.18) * values
    return jnp.clip(values, min=-bound, max=bound).astype(held_as)


def setup_inputs(seed: int = 0) -> dict:
    key_of = jax.random.split(jax.random.key(seed), 8)
    return {
        "query": draw_query(jax.random.fold_in(key_of[7], 71), 0),
        "page_owner": draw_page_owner(jax.random.fold_in(key_of[7], 71), 0),
        "page_fill": draw_page_fill(jax.random.fold_in(key_of[7], 71), 0),
        "cache": draw_cache(jax.random.fold_in(key_of[7], 71), 0),
        "w_uk": scatter_about(key_of[4], (H, NOPE, LATENT), NOPE ** -0.5, 0.5, ((0, 4),)),
        "w_uv": scatter_about(key_of[5], (H, LATENT, VDIM), LATENT ** -0.5, 0.25, ((0, 4),)),
        "w_out": scatter_about(key_of[6], (H * VDIM, D), (H * VDIM) ** -0.5, 0.125, ((0, 4),)),
    }


def page_scores(page_queries, block, fill):
    softmax_scale = 1.0 / math.sqrt(NOPE + ROPE)
    scores = jnp.einsum('phc,ptc->pht', page_queries.astype(jnp.float32), block.astype(jnp.float32)) * softmax_scale
    usable = jnp.arange(PAGE)[None, None, :] < fill[:, None, None]
    return (jnp.where(usable, scores, -1e+30), usable)

def reference(query, page_owner, page_fill, cache, w_uk, w_uv, w_out):
    shaped = query.reshape(REQUESTS, H, NOPE + ROPE)
    latent_q = jnp.einsum('rhn,hnc->rhc', shaped[:, :, :NOPE].astype(jnp.float32), w_uk.astype(jnp.float32)).astype(jnp.bfloat16)
    latent_q = lax.optimization_barrier(latent_q)
    joined = jnp.concatenate([latent_q, shaped[:, :, NOPE:]], axis=2)
    page_queries = jnp.take(joined, page_owner, axis=0)
    blocks = PAGES // PAGES_DEV
    query_blocks = page_queries.reshape(blocks, PAGES_DEV, H, LATENT + ROPE)
    cache_blocks = cache.reshape(blocks, PAGES_DEV, PAGE, LATENT + ROPE)
    fill_blocks = page_fill.reshape(blocks, PAGES_DEV)

    def block_peak(items):
        scores, usable = page_scores(items[0], items[1], items[2])
        return lax.optimization_barrier(jnp.max(scores, axis=2))
    page_peak = lax.map(block_peak, (query_blocks, cache_blocks, fill_blocks)).reshape(PAGES, H)
    member = page_owner[None, :] == jnp.arange(REQUESTS).astype(jnp.int32)[:, None]
    peak = lax.optimization_barrier(jnp.max(jnp.where(member[:, :, None], page_peak[None], -1e+30), axis=1))
    peak_blocks = jnp.take(peak, page_owner, axis=0).reshape(blocks, PAGES_DEV, H)

    def block_sums(items):
        scores, usable = page_scores(items[0], items[1], items[2])
        weights = jnp.where(usable, jnp.exp(scores - items[3][:, :, None]), 0.0)
        rounded = lax.optimization_barrier(weights.astype(jnp.bfloat16)).astype(jnp.float32)
        values = jnp.einsum('pht,ptc->phc', rounded, items[1][:, :, :LATENT].astype(jnp.float32))
        return (lax.optimization_barrier(jnp.sum(weights, axis=2)), values)
    totals, values = lax.map(block_sums, (query_blocks, cache_blocks, fill_blocks, peak_blocks))
    totals = totals.reshape(PAGES, H)
    values = values.reshape(PAGES, H, LATENT)
    member_f = member.astype(jnp.float32)
    denominator = jnp.dot(member_f, totals, precision=lax.Precision.HIGHEST)
    numerator = jnp.einsum('rp,phc->rhc', member_f, values, precision=lax.Precision.HIGHEST)
    attended = (numerator / denominator[:, :, None]).astype(jnp.bfloat16)
    head_out = jnp.einsum('rhc,hcv->rhv', attended.astype(jnp.float32), w_uv.astype(jnp.float32)).astype(jnp.bfloat16)
    head_out = head_out.reshape(REQUESTS, H * VDIM)
    return jnp.dot(head_out, w_out, preferred_element_type=jnp.float32).astype(jnp.bfloat16)
```

```python
import math

import jax
import jax.numpy as jnp
from jax import lax
from jax.experimental import pallas as pl
from jax.experimental.pallas import tpu as pltpu
from jax.sharding import PartitionSpec as P

MESH = pl.DeviceIdType.MESH
EMPTY = -1e30
LANES = 128
ROWS = 8
SENT = 6


def kernel(
    seq, tensor, scale,
    owner, fill, q_ref, cache_hbm, wuk_hbm, wuv_hbm, wout_hbm,
    out_ref,
    qall, cache, wuk, wuv, wout, sel, pick, sendb, recvb, rf, xs, xr,
    local_sems, qsend, qrecv, bsend, brecv, xsend, xrecv,
):
    pages, page, width = cache.shape
    heads, nope, latent = wuk.shape
    rope = width - latent
    tokens = pages * page
    me = lax.axis_index("seq")
    tx = lax.axis_index("tensor")
    barrier = pltpu.get_barrier_semaphore()

    def greet(k, c):
        pl.semaphore_signal(
            barrier, 1, device_id={"seq": lax.rem(me + k, seq)}, device_id_type=MESH
        )
        return c

    lax.fori_loop(1, seq, greet, 0)
    for k in range(1, tensor):
        pl.semaphore_signal(
            barrier, 1, device_id={"tensor": lax.rem(tx + k, tensor)}, device_id_type=MESH
        )
    loads = [
        pltpu.make_async_copy(src, dst, local_sems.at[i])
        for i, (src, dst) in enumerate(
            ((wuk_hbm, wuk), (cache_hbm, cache), (wuv_hbm, wuv), (wout_hbm, wout))
        )
    ]
    for load in loads:
        load.start()

    q = q_ref[...].astype(jnp.float32)
    step = nope + rope
    rows = [q[:, h * step : h * step + nope] for h in range(heads)]
    ropes = [q[:, h * step + nope : (h + 1) * step] for h in range(heads)]
    rows += [jnp.concatenate(ropes[h : h + 2], axis=1) for h in range(0, heads, 2)]
    rows += [jnp.zeros((ROWS - SENT, LANES), jnp.float32)]
    qall[me] = jnp.concatenate(rows, axis=0).astype(jnp.bfloat16)

    pl.semaphore_wait(barrier, seq - 1 + tensor - 1)

    def send_query(k, c):
        pltpu.make_async_remote_copy(
            src_ref=qall.at[me, pl.ds(0, SENT)],
            dst_ref=qall.at[me, pl.ds(0, SENT)],
            send_sem=qsend,
            recv_sem=qrecv,
            device_id={"seq": lax.rem(me + k, seq)},
            device_id_type=MESH,
        ).start()
        return c

    lax.fori_loop(1, seq, send_query, 0)

    row16 = lax.broadcasted_iota(jnp.int32, (pages, LANES), 0)
    lane16 = lax.broadcasted_iota(jnp.int32, (pages, LANES), 1)
    own_row = jnp.zeros((pages, LANES), jnp.int32)
    own_lane = jnp.zeros((pages, LANES), jnp.int32)
    for p in range(pages):
        own_row = jnp.where(row16 == p, owner[p], own_row)
        own_lane = jnp.where((lane16 & (pages - 1)) == p, owner[p], own_lane)
    repeated = jnp.max(
        jnp.where((own_row == own_lane) & (row16 < (lane16 & (pages - 1))), 1, 0),
        axis=0, keepdims=True,
    )
    first_lane = jnp.where(repeated > 0, -1, own_lane[:1])
    big_row = lax.broadcasted_iota(jnp.int32, (seq * ROWS, LANES), 0)
    big_lane = lax.broadcasted_iota(jnp.int32, (seq * ROWS, LANES), 1)
    wanted = (first_lane * ROWS) + lax.div(big_lane[:1], pages)
    wanted = jnp.where((first_lane >= 0) & (big_lane[:1] < (heads + 1) * pages), wanted, -1)
    pick[...] = jnp.where(big_row == wanted, 1.0, 0.0).astype(jnp.bfloat16)

    pltpu.make_async_copy(
        qall.at[pl.ds(0, seq - 1), pl.ds(0, SENT)],
        qall.at[pl.ds(0, seq - 1), pl.ds(0, SENT)],
        qrecv,
    ).wait()
    for p in range(pages):
        sel[p * ROWS : (p + 1) * ROWS, :] = qall[owner[p]].astype(jnp.float32)
    loads[0].wait()
    joined = []
    for h in range(heads):
        plain = sel[pl.ds(h, pages, stride=ROWS), :].astype(jnp.bfloat16)
        pair = sel[pl.ds(heads + h // 2, pages, stride=ROWS), :]
        turned = pair[:, (h % 2) * rope : (h % 2 + 1) * rope].astype(jnp.bfloat16)
        lat = jnp.dot(plain, wuk[h], preferred_element_type=jnp.float32).astype(jnp.bfloat16)
        joined.append(jnp.concatenate([lat, turned], axis=1))
    joined = jnp.concatenate(joined, axis=0)

    loads[1].wait()
    keys = cache[...].reshape(tokens, width)
    scores = lax.dot_general(
        joined, keys, (((1,), (1,)), ((), ())), preferred_element_type=jnp.float32
    )
    own_rows = jnp.concatenate([own_row] * heads, axis=0)
    lane = lax.broadcasted_iota(jnp.int32, (1, LANES), 1)
    per = LANES // page
    valid, kept = [], []
    for j in range(tokens // LANES):
        own_l = jnp.where(lane < page, owner[per * j], owner[per * j + 1])
        fill_l = jnp.where(lane < page, fill[per * j], fill[per * j + 1])
        own_l = jnp.where((lane & (page - 1)) < fill_l, own_l, -1)
        ok = own_rows == own_l
        valid.append(ok)
        kept.append(jnp.where(ok, scores[:, j * LANES : (j + 1) * LANES] * scale, EMPTY))
    top = kept[0]
    for part in kept[1:]:
        top = jnp.maximum(top, part)
    top = jnp.max(top, axis=1, keepdims=True)
    top = jnp.where(top > 0.5 * EMPTY, top, 0.0)
    top_hi = top.astype(jnp.bfloat16).astype(jnp.float32)
    top_lo = (top - top_hi).astype(jnp.bfloat16).astype(jnp.float32)
    shift = top_hi + top_lo
    weights = [jnp.where(ok, jnp.exp(s - shift), 0.0) for ok, s in zip(valid, kept)]
    total = weights[0]
    for part in weights[1:]:
        total = total + part
    total = jnp.sum(total, axis=1, keepdims=True)
    total_hi = total.astype(jnp.bfloat16).astype(jnp.float32)
    total_lo = total - total_hi
    weights = jnp.concatenate([w.astype(jnp.bfloat16) for w in weights], axis=1)
    sums = jnp.dot(weights, keys[:, :latent], preferred_element_type=jnp.float32)

    loads[2].wait()
    blocks = [
        jnp.dot(
            sums[h * pages : (h + 1) * pages].astype(jnp.bfloat16), wuv[h],
            preferred_element_type=jnp.float32,
        )
        for h in range(heads)
    ]
    stats = jnp.zeros((pages, LANES), jnp.float32)
    for i, part in enumerate((top_hi, top_lo, total_hi, total_lo)):
        for h in range(heads):
            stats = jnp.where(
                lane16 == i * heads + h, part[h * pages : (h + 1) * pages], stats
            )
    blocks += [stats, jnp.zeros((LANES - (heads + 1) * pages, LANES), jnp.float32)]
    table = jnp.concatenate(blocks, axis=0).astype(jnp.bfloat16)
    sendb[...] = (
        jnp.dot(pick[...], table, preferred_element_type=jnp.float32)
        .astype(jnp.bfloat16)
        .reshape(seq, ROWS, LANES)
    )
    recvb[me] = sendb[me]

    def send_sums(k, c):
        peer = lax.rem(me + k, seq)
        pltpu.make_async_remote_copy(
            src_ref=sendb.at[peer, pl.ds(0, SENT)],
            dst_ref=recvb.at[me, pl.ds(0, SENT)],
            send_sem=bsend,
            recv_sem=brecv,
            device_id={"seq": peer},
            device_id_type=MESH,
        ).start()
        return c

    lax.fori_loop(1, seq, send_sums, 0)
    pltpu.make_async_copy(
        recvb.at[pl.ds(0, seq - 1), pl.ds(0, SENT)],
        recvb.at[pl.ds(0, seq - 1), pl.ds(0, SENT)],
        brecv,
    ).wait()

    rf[...] = recvb[...].reshape(seq * ROWS, LANES).astype(jnp.float32)
    got = rf[pl.ds(heads, seq, stride=ROWS), :]
    tops = got + pltpu.roll(got, LANES - heads, 1)
    totals = pltpu.roll(got, LANES - 2 * heads, 1) + pltpu.roll(got, LANES - 3 * heads, 1)
    some = totals > 0.0
    tops = jnp.where(some, tops, EMPTY)
    peak = jnp.max(tops, axis=0, keepdims=True)
    share = jnp.where(some, jnp.exp(tops - peak), 0.0)
    denominator = jnp.sum(jnp.where(some, share * totals, 0.0), axis=0, keepdims=True)
    outs = []
    for h in range(heads):
        mine = rf[pl.ds(h, seq, stride=ROWS), :]
        numerator = jnp.sum(mine * share[:, h : h + 1], axis=0, keepdims=True)
        outs.append(numerator / denominator[:, h : h + 1])
    head_out = jnp.concatenate(outs, axis=1).astype(jnp.bfloat16)

    loads[3].wait()
    partial_value = jnp.dot(head_out, wout[...], preferred_element_type=jnp.float32)
    columns = partial_value.shape[1] // tensor
    for t in range(tensor):
        xs[t] = partial_value[:, t * columns : (t + 1) * columns]
    xr[tx] = xs[tx]
    sends = []
    for k in range(1, tensor):
        peer = lax.rem(tx + k, tensor)
        sends.append(
            pltpu.make_async_remote_copy(
                src_ref=xs.at[peer],
                dst_ref=xr.at[tx],
                send_sem=xsend.at[k],
                recv_sem=xrecv.at[k],
                device_id={"tensor": peer},
                device_id_type=MESH,
            )
        )
    for send in sends:
        send.start()
    for send in sends:
        send.wait_recv()
    total_value = xr[0]
    for t in range(1, tensor):
        total_value = total_value + xr[t]
    out_ref[...] = total_value.astype(out_ref.dtype)
    for send in sends:
        send.wait_send()
    for ref, sem in ((qall, qsend), (sendb, bsend)):
        pltpu.make_async_copy(
            ref.at[pl.ds(0, seq - 1), pl.ds(0, SENT)],
            ref.at[pl.ds(0, seq - 1), pl.ds(0, SENT)],
            sem,
        ).wait()


def solution(mesh):
    seq, tensor = mesh.shape["seq"], mesh.shape["tensor"]

    def shards(query, page_owner, page_fill, cache, w_uk, w_uv, w_out):
        heads = w_uk.shape[0]
        width = query.shape[1] // heads
        columns = w_out.shape[1] // tensor

        def body(*refs):
            kernel(seq, tensor, 1.0 / math.sqrt(width), *refs)

        smem = pl.BlockSpec(memory_space=pltpu.SMEM)
        vmem = pl.BlockSpec(memory_space=pltpu.VMEM)
        hbm = pl.BlockSpec(memory_space=pl.ANY)
        dma = pltpu.SemaphoreType.DMA
        return pl.pallas_call(
            body,
            out_shape=jax.ShapeDtypeStruct((query.shape[0], columns), jnp.bfloat16),
            in_specs=[smem, smem, vmem, hbm, hbm, hbm, hbm],
            out_specs=vmem,
            scratch_shapes=[
                pltpu.VMEM((seq, ROWS, LANES), jnp.bfloat16),
                pltpu.VMEM(cache.shape, cache.dtype),
                pltpu.VMEM(w_uk.shape, w_uk.dtype),
                pltpu.VMEM(w_uv.shape, w_uv.dtype),
                pltpu.VMEM(w_out.shape, w_out.dtype),
                pltpu.VMEM((page_owner.shape[0] * ROWS, LANES), jnp.float32),
                pltpu.VMEM((seq * ROWS, LANES), jnp.bfloat16),
                pltpu.VMEM((seq, ROWS, LANES), jnp.bfloat16),
                pltpu.VMEM((seq, ROWS, LANES), jnp.bfloat16),
                pltpu.VMEM((seq * ROWS, LANES), jnp.float32),
                pltpu.VMEM((tensor, 1, columns), jnp.float32),
                pltpu.VMEM((tensor, 1, columns), jnp.float32),
                dma((4,)),
                dma, dma, dma, dma,
                dma((tensor,)),
                dma((tensor,)),
            ],
            compiler_params=pltpu.CompilerParams(collective_id=0, has_side_effects=True),
        )(page_owner, page_fill, query, cache, w_uk, w_uv, w_out)

    return jax.shard_map(
        shards,
        mesh=mesh,
        in_specs=(
            P("seq", "tensor"), P("seq"), P("seq"), P("seq", None, None),
            P("tensor", None, None), P("tensor", None, None), P("tensor", None),
        ),
        out_specs=P("seq", "tensor"),
        check_vma=False,
    )
```

```python
import math

import jax
import jax.numpy as jnp
from jax import lax
from jax.experimental import pallas as pl
from jax.experimental.pallas import tpu as pltpu
from jax.sharding import PartitionSpec as P

MESH = pl.DeviceIdType.MESH
EMPTY = -1e30
LANES = 128
ROWS = 8
SENT = 6
NY = 8


def kernel(
    seq, tensor, scale, ny, nz,
    owner, fill, q_ref, cache_hbm, wuk_hbm, wuv_hbm, wout_hbm,
    out_ref,
    qmine, qearly, qlate, cache, wuk, wuv, wout, bias, sel, pick, sendb, recvb, rf, xs, xr,
    local_sems, send1, recv1, send2, recv2, bsend, brecv, xsend, xrecv,
):
    pages, page, width = cache.shape
    heads, nope, latent = wuk.shape
    rope = width - latent
    tokens = pages * page
    me = lax.axis_index("seq")
    tx = lax.axis_index("tensor")
    core = lax.rem(me, 2)
    y = lax.rem(lax.div(me, 2), ny)
    z = lax.div(me, 2 * ny)
    line = y * 2 + core
    deep = nz // 2
    late = lax.div(z, deep)
    slot = line * deep + lax.rem(z, deep)
    half = seq // 2

    def seat(z_at, line_at):
        return z_at * (2 * ny) + line_at

    def along_z(k):
        return seat(lax.rem(z + k, nz), line)

    def along_y(k):
        return seat(z, lax.rem(line + k, 2 * ny))

    barrier = pltpu.get_barrier_semaphore()
    for k in range(1, nz):
        pl.semaphore_signal(barrier, 1, device_id={"seq": along_z(k)}, device_id_type=MESH)
    for k in range(1, 2 * ny):
        pl.semaphore_signal(barrier, 1, device_id={"seq": along_y(k)}, device_id_type=MESH)
    for k in range(1, tensor):
        pl.semaphore_signal(
            barrier, 1, device_id={"tensor": lax.rem(tx + k, tensor)}, device_id_type=MESH
        )

    q = q_ref[...].astype(jnp.float32)
    step = nope + rope
    rows = [q[:, h * step : h * step + nope] for h in range(heads)]
    ropes = [q[:, h * step + nope : (h + 1) * step] for h in range(heads)]
    rows += [jnp.concatenate(ropes[h : h + 2], axis=1) for h in range(0, heads, 2)]
    rows += [jnp.zeros((ROWS - SENT, LANES), jnp.float32)]
    qmine[...] = jnp.concatenate(rows, axis=0).astype(jnp.bfloat16)[None]
    loads = [
        pltpu.make_async_copy(src, dst, local_sems.at[i])
        for i, (src, dst) in enumerate(
            ((wuk_hbm, wuk), (cache_hbm, cache), (wuv_hbm, wuv), (wout_hbm, wout))
        )
    ]
    queries = (qearly, qlate)
    sent = pl.ds(0, SENT)

    pl.semaphore_wait(barrier, nz - 1 + 2 * ny - 1 + tensor - 1)

    for part, buf in enumerate(queries):

        @pl.when(late == part)
        def _(part=part, buf=buf):
            for k in range(1, nz):
                pltpu.make_async_remote_copy(
                    src_ref=qmine.at[:, sent],
                    dst_ref=buf.at[pl.ds(slot, 1), sent],
                    send_sem=send1,
                    recv_sem=recv1.at[part],
                    device_id={"seq": along_z(k)},
                    device_id_type=MESH,
                ).start()
            pltpu.make_async_copy(
                qmine.at[:, sent], buf.at[pl.ds(slot, 1), sent], recv1.at[part]
            ).start()

    for load in loads:
        load.start()

    row16 = lax.broadcasted_iota(jnp.int32, (pages, LANES), 0)
    lane16 = lax.broadcasted_iota(jnp.int32, (pages, LANES), 1)
    own_row = jnp.zeros((pages, LANES), jnp.int32)
    own_lane = jnp.zeros((pages, LANES), jnp.int32)
    for p in range(pages):
        own_row = jnp.where(row16 == p, owner[p], own_row)
        own_lane = jnp.where((lane16 & (pages - 1)) == p, owner[p], own_lane)
    repeated = jnp.max(
        jnp.where((own_row == own_lane) & (row16 < (lane16 & (pages - 1))), 1, 0),
        axis=0, keepdims=True,
    )
    first_lane = jnp.where(repeated > 0, -1, own_lane[:1])
    big_row = lax.broadcasted_iota(jnp.int32, (seq * ROWS, LANES), 0)
    big_lane = lax.broadcasted_iota(jnp.int32, (seq * ROWS, LANES), 1)
    wanted = (first_lane * ROWS) + lax.div(big_lane[:1], pages)
    wanted = jnp.where((first_lane >= 0) & (big_lane[:1] < (heads + 1) * pages), wanted, -1)
    pick[...] = jnp.where(big_row == wanted, 1.0, 0.0).astype(jnp.bfloat16)
    own_rows = jnp.concatenate([own_row] * heads, axis=0)
    lane = lax.broadcasted_iota(jnp.int32, (1, LANES), 1)
    per = LANES // page
    for j in range(tokens // LANES):
        own_l = jnp.where(lane < page, owner[per * j], owner[per * j + 1])
        fill_l = jnp.where(lane < page, fill[per * j], fill[per * j + 1])
        own_l = jnp.where((lane & (page - 1)) < fill_l, own_l, -1)
        bias[:, j * LANES : (j + 1) * LANES] = jnp.where(own_rows == own_l, 0.0, EMPTY)

    for part, buf in enumerate(queries):
        whole = buf.at[pl.ds(0, deep), sent]
        pltpu.make_async_copy(whole, whole, recv1.at[part]).wait()
        mine = buf.at[pl.ds(line * deep, deep), sent]
        for k in range(1, 2 * ny):
            pltpu.make_async_remote_copy(
                src_ref=mine,
                dst_ref=mine,
                send_sem=send2,
                recv_sem=recv2.at[part],
                device_id={"seq": along_y(k)},
                device_id_type=MESH,
            ).start()

    for part, buf in enumerate(queries):
        rest = buf.at[pl.ds(0, (2 * ny - 1) * deep), sent]
        pltpu.make_async_copy(rest, rest, recv2.at[part]).wait()
        for p in range(pages):
            at = (owner[p] & (2 * ny - 1)) * deep + ((owner[p] // (2 * ny)) & (deep - 1))
            sel[p * ROWS : (p + 1) * ROWS, :] = buf[at].astype(jnp.float32)
        if part == 0:
            loads[0].wait()
        joined = []
        for h in range(heads):
            plain = sel[pl.ds(h, pages, stride=ROWS), :].astype(jnp.bfloat16)
            pair = sel[pl.ds(heads + h // 2, pages, stride=ROWS), :]
            turned = pair[:, (h % 2) * rope : (h % 2 + 1) * rope].astype(jnp.bfloat16)
            lat = jnp.dot(plain, wuk[h], preferred_element_type=jnp.float32)
            joined.append(jnp.concatenate([lat.astype(jnp.bfloat16), turned], axis=1))
        joined = jnp.concatenate(joined, axis=0)

        if part == 0:
            loads[1].wait()
        keys = cache[...].reshape(tokens, width)
        scores = lax.dot_general(
            joined, keys, (((1,), (1,)), ((), ())), preferred_element_type=jnp.float32
        )
        scores = scores * scale + bias[...]
        top = jnp.max(scores, axis=1, keepdims=True)
        top = jnp.where(top > 0.5 * EMPTY, top, 0.0)
        top_hi = top.astype(jnp.bfloat16).astype(jnp.float32)
        top_lo = (top - top_hi).astype(jnp.bfloat16).astype(jnp.float32)
        weights = jnp.exp(scores - (top_hi + top_lo))
        total = jnp.sum(weights, axis=1, keepdims=True)
        total_hi = total.astype(jnp.bfloat16).astype(jnp.float32)
        total_lo = total - total_hi
        sums = jnp.dot(
            weights.astype(jnp.bfloat16), keys[:, :latent], preferred_element_type=jnp.float32
        )

        if part == 0:
            loads[2].wait()
        blocks = [
            jnp.dot(
                sums[h * pages : (h + 1) * pages].astype(jnp.bfloat16), wuv[h],
                preferred_element_type=jnp.float32,
            )
            for h in range(heads)
        ]
        stats = jnp.zeros((pages, LANES), jnp.float32)
        for i, piece in enumerate((top_hi, top_lo, total_hi, total_lo)):
            for h in range(heads):
                stats = jnp.where(
                    lane16 == i * heads + h, piece[h * pages : (h + 1) * pages], stats
                )
        blocks += [stats, jnp.zeros((LANES - (heads + 1) * pages, LANES), jnp.float32)]
        table = jnp.concatenate(blocks, axis=0).astype(jnp.bfloat16)
        sendb[pl.ds(part * half, half)] = (
            jnp.dot(
                pick[pl.ds(part * half * ROWS, half * ROWS), :], table,
                preferred_element_type=jnp.float32,
            )
            .astype(jnp.bfloat16)
            .reshape(half, ROWS, LANES)
        )

        def send_sums(k, c, part=part):
            peer = part * half + lax.rem(me + k, half)
            pltpu.make_async_remote_copy(
                src_ref=sendb.at[peer, sent],
                dst_ref=recvb.at[me, sent],
                send_sem=bsend,
                recv_sem=brecv,
                device_id={"seq": peer},
                device_id_type=MESH,
            ).start()
            return c

        lax.fori_loop(jnp.where(late == part, 1, 0), half, send_sums, 0)

    recvb[me] = sendb[me]
    others = recvb.at[pl.ds(0, seq - 1), sent]
    pltpu.make_async_copy(others, others, brecv).wait()

    rf[...] = recvb[...].reshape(seq * ROWS, LANES).astype(jnp.float32)
    got = rf[pl.ds(heads, seq, stride=ROWS), :]
    tops = got + pltpu.roll(got, LANES - heads, 1)
    totals = pltpu.roll(got, LANES - 2 * heads, 1) + pltpu.roll(got, LANES - 3 * heads, 1)
    some = totals > 0.0
    tops = jnp.where(some, tops, EMPTY)
    peak = jnp.max(tops, axis=0, keepdims=True)
    share = jnp.where(some, jnp.exp(tops - peak), 0.0)
    denominator = jnp.sum(jnp.where(some, share * totals, 0.0), axis=0, keepdims=True)
    outs = []
    for h in range(heads):
        mine = rf[pl.ds(h, seq, stride=ROWS), :]
        numerator = jnp.sum(mine * share[:, h : h + 1], axis=0, keepdims=True)
        outs.append(numerator / denominator[:, h : h + 1])
    head_out = jnp.concatenate(outs, axis=1).astype(jnp.bfloat16)

    loads[3].wait()
    partial_value = jnp.dot(head_out, wout[...], preferred_element_type=jnp.float32)
    columns = partial_value.shape[1] // tensor
    for t in range(tensor):
        xs[t] = partial_value[:, t * columns : (t + 1) * columns]
    xr[tx] = xs[tx]
    sends = []
    for k in range(1, tensor):
        peer = lax.rem(tx + k, tensor)
        sends.append(
            pltpu.make_async_remote_copy(
                src_ref=xs.at[peer],
                dst_ref=xr.at[tx],
                send_sem=xsend.at[k],
                recv_sem=xrecv.at[k],
                device_id={"tensor": peer},
                device_id_type=MESH,
            )
        )
    for send in sends:
        send.start()
    for send in sends:
        send.wait_recv()
    total_value = xr[0]
    for t in range(1, tensor):
        total_value = total_value + xr[t]
    out_ref[...] = total_value.astype(out_ref.dtype)
    for send in sends:
        send.wait_send()
    away = qearly.at[pl.ds(0, nz - 1), sent]
    pltpu.make_async_copy(away, away, send1).wait()
    for buf in queries:
        away = buf.at[pl.ds(0, (2 * ny - 1) * deep), sent]
        pltpu.make_async_copy(away, away, send2).wait()
    away = sendb.at[pl.ds(0, seq - 1), sent]
    pltpu.make_async_copy(away, away, bsend).wait()


def solution(mesh):
    seq, tensor = mesh.shape["seq"], mesh.shape["tensor"]

    def shards(query, page_owner, page_fill, cache, w_uk, w_uv, w_out):
        heads = w_uk.shape[0]
        width = query.shape[1] // heads
        columns = w_out.shape[1] // tensor
        ny = NY

        def body(*refs):
            kernel(seq, tensor, 1.0 / math.sqrt(width), ny, seq // (2 * ny), *refs)

        smem = pl.BlockSpec(memory_space=pltpu.SMEM)
        vmem = pl.BlockSpec(memory_space=pltpu.VMEM)
        hbm = pl.BlockSpec(memory_space=pl.ANY)
        dma = pltpu.SemaphoreType.DMA
        return pl.pallas_call(
            body,
            out_shape=jax.ShapeDtypeStruct((query.shape[0], columns), jnp.bfloat16),
            in_specs=[smem, smem, vmem, hbm, hbm, hbm, hbm],
            out_specs=vmem,
            scratch_shapes=[
                pltpu.VMEM((1, ROWS, LANES), jnp.bfloat16),
                pltpu.VMEM((seq // 2, ROWS, LANES), jnp.bfloat16),
                pltpu.VMEM((seq // 2, ROWS, LANES), jnp.bfloat16),
                pltpu.VMEM(cache.shape, cache.dtype),
                pltpu.VMEM(w_uk.shape, w_uk.dtype),
                pltpu.VMEM(w_uv.shape, w_uv.dtype),
                pltpu.VMEM(w_out.shape, w_out.dtype),
                pltpu.VMEM((page_owner.shape[0] * heads, cache.shape[0] * cache.shape[1]), jnp.float32),
                pltpu.VMEM((page_owner.shape[0] * ROWS, LANES), jnp.float32),
                pltpu.VMEM((seq * ROWS, LANES), jnp.bfloat16),
                pltpu.VMEM((seq, ROWS, LANES), jnp.bfloat16),
                pltpu.VMEM((seq, ROWS, LANES), jnp.bfloat16),
                pltpu.VMEM((seq * ROWS, LANES), jnp.float32),
                pltpu.VMEM((tensor, 1, columns), jnp.float32),
                pltpu.VMEM((tensor, 1, columns), jnp.float32),
                dma((4,)),
                dma,
                dma((2,)),
                dma,
                dma((2,)),
                dma, dma,
                dma((tensor,)),
                dma((tensor,)),
            ],
            compiler_params=pltpu.CompilerParams(collective_id=0, has_side_effects=True),
        )(page_owner, page_fill, query, cache, w_uk, w_uv, w_out)

    return jax.shard_map(
        shards,
        mesh=mesh,
        in_specs=(
            P("seq", "tensor"), P("seq"), P("seq"), P("seq", None, None),
            P("tensor", None, None), P("tensor", None, None), P("tensor", None),
        ),
        out_specs=P("seq", "tensor"),
        check_vma=False,
    )
```

```python
import functools
import math

import jax
import jax.numpy as jnp
from jax import lax
from jax.experimental import pallas as pl
from jax.experimental.pallas import tpu as pltpu
from jax.sharding import PartitionSpec as P

MESH = pl.DeviceIdType.MESH
EMPTY = -1e30
LANES = 128
ROWS = 8
SENT = 6
NY = 8


def kernel(
    seq, tensor, scale, ny, nz,
    owner_hbm, fill_hbm, q_hbm, cache_hbm, wuk_hbm, wuv_hbm, wout_hbm,
    out_ref,
    owner, fill, q_ref, qmine, qearly, qlate, cache, wuk, wuv, wout, bias, sel, pick, sendb, recvb, rf, xs, xr,
    local_sems, send1, recv1, send2, recv2, bsend, brecv, xsend, xrecv,
):
    pages, page, width = cache.shape
    heads, nope, latent = wuk.shape
    rope = width - latent
    tokens = pages * page
    columns = wout.shape[2]
    me = lax.axis_index("seq")
    tx = lax.axis_index("tensor")
    core = lax.rem(me, 2)
    y = lax.rem(lax.div(me, 2), ny)
    z = lax.div(me, 2 * ny)
    line = y * 2 + core
    deep = nz // 2
    late = lax.div(z, deep)
    slot = line * deep + lax.rem(z, deep)
    half = seq // 2

    def seat(z_at, line_at):
        return z_at * (2 * ny) + line_at

    def along_z(k):
        return seat(lax.rem(z + k, nz), line)

    def along_y(k):
        return seat(z, lax.rem(line + k, 2 * ny))

    small = [
        pltpu.make_async_copy(src, dst, local_sems.at[i])
        for i, (src, dst) in enumerate(((q_hbm, q_ref), (owner_hbm, owner), (fill_hbm, fill)))
    ]
    small[0].start()

    barrier = pltpu.get_barrier_semaphore()
    for k in range(1, nz):
        pl.semaphore_signal(barrier, 1, device_id={"seq": along_z(k)}, device_id_type=MESH)
    for k in range(1, 2 * ny):
        pl.semaphore_signal(barrier, 1, device_id={"seq": along_y(k)}, device_id_type=MESH)
    for k in range(1, tensor):
        pl.semaphore_signal(
            barrier, 1, device_id={"tensor": lax.rem(tx + k, tensor)}, device_id_type=MESH
        )

    small[1].start()
    small[2].start()

    small[0].wait()
    q = q_ref[...].astype(jnp.float32)
    step = nope + rope
    rows = [q[:, h * step : h * step + nope] for h in range(heads)]
    ropes = [q[:, h * step + nope : (h + 1) * step] for h in range(heads)]
    rows += [jnp.concatenate(ropes[h : h + 2], axis=1) for h in range(0, heads, 2)]
    rows += [jnp.zeros((ROWS - SENT, LANES), jnp.float32)]
    qmine[...] = jnp.concatenate(rows, axis=0).astype(jnp.bfloat16)[None]
    loads = [
        pltpu.make_async_copy(src, dst, local_sems.at[3 + i])
        for i, (src, dst) in enumerate(
            ((wuk_hbm, wuk), (cache_hbm, cache), (wuv_hbm, wuv))
            + tuple((wout_hbm.at[:, pl.ds(t * columns, columns)], wout.at[t]) for t in range(tensor))
        )
    ]
    queries = (qearly, qlate)
    sent = pl.ds(0, SENT)

    pl.semaphore_wait(barrier, nz - 1 + 2 * ny - 1 + tensor - 1)

    for part, buf in enumerate(queries):

        @pl.when(late == part)
        def _(part=part, buf=buf):
            for k in range(1, nz):
                pltpu.make_async_remote_copy(
                    src_ref=qmine.at[:, sent],
                    dst_ref=buf.at[pl.ds(slot, 1), sent],
                    send_sem=send1,
                    recv_sem=recv1.at[part],
                    device_id={"seq": along_z(k)},
                    device_id_type=MESH,
                ).start()
            pltpu.make_async_copy(
                qmine.at[:, sent], buf.at[pl.ds(slot, 1), sent], recv1.at[part]
            ).start()

    for load in loads:
        load.start()

    small[1].wait()
    small[2].wait()
    row16 = lax.broadcasted_iota(jnp.int32, (pages, LANES), 0)
    lane16 = lax.broadcasted_iota(jnp.int32, (pages, LANES), 1)
    own_row = jnp.zeros((pages, LANES), jnp.int32)
    own_lane = jnp.zeros((pages, LANES), jnp.int32)
    for p in range(pages):
        own_row = jnp.where(row16 == p, owner[p], own_row)
        own_lane = jnp.where((lane16 & (pages - 1)) == p, owner[p], own_lane)
    repeated = jnp.max(
        jnp.where((own_row == own_lane) & (row16 < (lane16 & (pages - 1))), 1, 0),
        axis=0, keepdims=True,
    )
    first_lane = jnp.where(repeated > 0, -1, own_lane[:1])
    big_row = lax.broadcasted_iota(jnp.int32, (seq * ROWS, LANES), 0)
    big_lane = lax.broadcasted_iota(jnp.int32, (seq * ROWS, LANES), 1)
    wanted = (first_lane * ROWS) + lax.div(big_lane[:1], pages)
    wanted = jnp.where((first_lane >= 0) & (big_lane[:1] < (heads + 1) * pages), wanted, -1)
    pick[...] = jnp.where(big_row == wanted, 1.0, 0.0).astype(jnp.bfloat16)
    own_rows = jnp.concatenate([own_row] * heads, axis=0)
    lane = lax.broadcasted_iota(jnp.int32, (1, LANES), 1)
    per = LANES // page
    for j in range(tokens // LANES):
        own_l = jnp.where(lane < page, owner[per * j], owner[per * j + 1])
        fill_l = jnp.where(lane < page, fill[per * j], fill[per * j + 1])
        own_l = jnp.where((lane & (page - 1)) < fill_l, own_l, -1)
        bias[:, j * LANES : (j + 1) * LANES] = jnp.where(own_rows == own_l, 0.0, EMPTY)

    for part, buf in enumerate(queries):
        whole = buf.at[pl.ds(0, deep), sent]
        pltpu.make_async_copy(whole, whole, recv1.at[part]).wait()
        mine = buf.at[pl.ds(line * deep, deep), sent]
        for k in range(1, 2 * ny):
            pltpu.make_async_remote_copy(
                src_ref=mine,
                dst_ref=mine,
                send_sem=send2,
                recv_sem=recv2.at[part],
                device_id={"seq": along_y(k)},
                device_id_type=MESH,
            ).start()

    for part, buf in enumerate(queries):
        rest = buf.at[pl.ds(0, (2 * ny - 1) * deep), sent]
        pltpu.make_async_copy(rest, rest, recv2.at[part]).wait()
        for p in range(pages):
            at = (owner[p] & (2 * ny - 1)) * deep + ((owner[p] // (2 * ny)) & (deep - 1))
            sel[p * ROWS : (p + 1) * ROWS, :] = buf[at].astype(jnp.float32)
        if part == 0:
            loads[0].wait()
        joined = []
        for h in range(heads):
            plain = sel[pl.ds(h, pages, stride=ROWS), :].astype(jnp.bfloat16)
            pair = sel[pl.ds(heads + h // 2, pages, stride=ROWS), :]
            turned = pair[:, (h % 2) * rope : (h % 2 + 1) * rope].astype(jnp.bfloat16)
            lat = jnp.dot(plain, wuk[h], preferred_element_type=jnp.float32)
            joined.append(jnp.concatenate([lat.astype(jnp.bfloat16), turned], axis=1))
        joined = jnp.concatenate(joined, axis=0)

        if part == 0:
            loads[1].wait()
        keys = cache[...].reshape(tokens, width)
        scores = lax.dot_general(
            joined, keys, (((1,), (1,)), ((), ())), preferred_element_type=jnp.float32
        )
        scores = scores * scale + bias[...]
        top = jnp.max(scores, axis=1, keepdims=True)
        top = jnp.where(top > 0.5 * EMPTY, top, 0.0)
        top_hi = top.astype(jnp.bfloat16).astype(jnp.float32)
        top_lo = (top - top_hi).astype(jnp.bfloat16).astype(jnp.float32)
        weights = jnp.exp(scores - (top_hi + top_lo))
        total = jnp.sum(weights, axis=1, keepdims=True)
        total_hi = total.astype(jnp.bfloat16).astype(jnp.float32)
        total_lo = total - total_hi
        sums = jnp.dot(
            weights.astype(jnp.bfloat16), keys[:, :latent], preferred_element_type=jnp.float32
        )

        if part == 0:
            loads[2].wait()
        blocks = [
            jnp.dot(
                sums[h * pages : (h + 1) * pages].astype(jnp.bfloat16), wuv[h],
                preferred_element_type=jnp.float32,
            )
            for h in range(heads)
        ]
        stats = jnp.zeros((pages, LANES), jnp.float32)
        for i, piece in enumerate((top_hi, top_lo, total_hi, total_lo)):
            for h in range(heads):
                stats = jnp.where(
                    lane16 == i * heads + h, piece[h * pages : (h + 1) * pages], stats
                )
        blocks += [stats, jnp.zeros((LANES - (heads + 1) * pages, LANES), jnp.float32)]
        table = jnp.concatenate(blocks, axis=0).astype(jnp.bfloat16)
        sendb[pl.ds(part * half, half)] = (
            jnp.dot(
                pick[pl.ds(part * half * ROWS, half * ROWS), :], table,
                preferred_element_type=jnp.float32,
            )
            .astype(jnp.bfloat16)
            .reshape(half, ROWS, LANES)
        )

        def send_sums(k, c, base):
            peer = base + lax.rem(line + k, 2 * ny)
            pltpu.make_async_remote_copy(
                src_ref=sendb.at[peer, sent],
                dst_ref=recvb.at[me, sent],
                send_sem=bsend,
                recv_sem=brecv,
                device_id={"seq": peer},
                device_id_type=MESH,
            ).start()
            return c

        for level in range(part * deep, (part + 1) * deep):
            lax.fori_loop(
                jnp.where(z == level, 1, 0), 2 * ny,
                functools.partial(send_sums, base=level * 2 * ny), 0,
            )

    recvb[me] = sendb[me]
    others = recvb.at[pl.ds(0, seq - 1), sent]
    pltpu.make_async_copy(others, others, brecv).wait()

    rf[...] = recvb[...].reshape(seq * ROWS, LANES).astype(jnp.float32)
    got = rf[pl.ds(heads, seq, stride=ROWS), :]
    tops = got + pltpu.roll(got, LANES - heads, 1)
    totals = pltpu.roll(got, LANES - 2 * heads, 1) + pltpu.roll(got, LANES - 3 * heads, 1)
    some = totals > 0.0
    tops = jnp.where(some, tops, EMPTY)
    peak = jnp.max(tops, axis=0, keepdims=True)
    share = jnp.where(some, jnp.exp(tops - peak), 0.0)
    denominator = jnp.sum(jnp.where(some, share * totals, 0.0), axis=0, keepdims=True)
    outs = []
    for h in range(heads):
        mine = rf[pl.ds(h, seq, stride=ROWS), :]
        numerator = jnp.sum(mine * share[:, h : h + 1], axis=0, keepdims=True)
        outs.append(numerator / denominator[:, h : h + 1])
    head_out = jnp.concatenate(outs, axis=1).astype(jnp.bfloat16)

    for load in loads[3:]:
        load.wait()
    sends = []
    for k in [2, 1, 3, 0]:
        peer = lax.rem(tx + k, tensor)
        piece = jnp.dot(head_out, wout[peer], preferred_element_type=jnp.float32)
        if k == 0:
            xr[tx] = piece
            continue
        xs[peer] = piece
        sends.append(
            pltpu.make_async_remote_copy(
                src_ref=xs.at[peer],
                dst_ref=xr.at[tx],
                send_sem=xsend.at[k],
                recv_sem=xrecv.at[k],
                device_id={"tensor": peer},
                device_id_type=MESH,
            )
        )
        sends[-1].start()
    for send in sends:
        send.wait_recv()
    total_value = xr[0]
    for t in range(1, tensor):
        total_value = total_value + xr[t]
    out_ref[...] = total_value.astype(out_ref.dtype)
    for send in sends:
        send.wait_send()
    away = qearly.at[pl.ds(0, nz - 1), sent]
    pltpu.make_async_copy(away, away, send1).wait()
    for buf in queries:
        away = buf.at[pl.ds(0, (2 * ny - 1) * deep), sent]
        pltpu.make_async_copy(away, away, send2).wait()
    away = sendb.at[pl.ds(0, seq - 1), sent]
    pltpu.make_async_copy(away, away, bsend).wait()


def solution(mesh):
    seq, tensor = mesh.shape["seq"], mesh.shape["tensor"]

    def shards(query, page_owner, page_fill, cache, w_uk, w_uv, w_out):
        heads = w_uk.shape[0]
        width = query.shape[1] // heads
        columns = w_out.shape[1] // tensor
        ny = NY

        def body(*refs):
            kernel(seq, tensor, 1.0 / math.sqrt(width), ny, seq // (2 * ny), *refs)

        vmem = pl.BlockSpec(memory_space=pltpu.VMEM)
        hbm = pl.BlockSpec(memory_space=pltpu.HBM)
        dma = pltpu.SemaphoreType.DMA
        return pl.pallas_call(
            body,
            out_shape=pltpu.VMEM((query.shape[0], columns), jnp.bfloat16),
            in_specs=[hbm] * 7,
            out_specs=vmem,
            scratch_shapes=[
                pltpu.SMEM(page_owner.shape, page_owner.dtype),
                pltpu.SMEM(page_fill.shape, page_fill.dtype),
                pltpu.VMEM(query.shape, query.dtype),
                pltpu.VMEM((1, ROWS, LANES), jnp.bfloat16),
                pltpu.VMEM((seq // 2, ROWS, LANES), jnp.bfloat16),
                pltpu.VMEM((seq // 2, ROWS, LANES), jnp.bfloat16),
                pltpu.VMEM(cache.shape, cache.dtype),
                pltpu.VMEM(w_uk.shape, w_uk.dtype),
                pltpu.VMEM(w_uv.shape, w_uv.dtype),
                pltpu.VMEM((tensor, w_out.shape[0], columns), w_out.dtype),
                pltpu.VMEM((page_owner.shape[0] * heads, cache.shape[0] * cache.shape[1]), jnp.float32),
                pltpu.VMEM((page_owner.shape[0] * ROWS, LANES), jnp.float32),
                pltpu.VMEM((seq * ROWS, LANES), jnp.bfloat16),
                pltpu.VMEM((seq, ROWS, LANES), jnp.bfloat16),
                pltpu.VMEM((seq, ROWS, LANES), jnp.bfloat16),
                pltpu.VMEM((seq * ROWS, LANES), jnp.float32),
                pltpu.VMEM((tensor, 1, columns), jnp.float32),
                pltpu.VMEM((tensor, 1, columns), jnp.float32),
                dma((10,)),
                dma,
                dma((2,)),
                dma,
                dma((2,)),
                dma, dma,
                dma((tensor,)),
                dma((tensor,)),
            ],
            compiler_params=pltpu.CompilerParams(collective_id=0, has_side_effects=True),
        )(page_owner, page_fill, query, cache, w_uk, w_uv, w_out)

    return jax.shard_map(
        shards,
        mesh=mesh,
        in_specs=(
            P("seq", "tensor"), P("seq"), P("seq"), P("seq", None, None),
            P("tensor", None, None), P("tensor", None, None), P("tensor", None),
        ),
        out_specs=P("seq", "tensor"),
        check_vma=False,
    )
```

```python
import functools
import math

import jax
import jax.numpy as jnp
from jax import lax
from jax.experimental import pallas as pl
from jax.experimental.pallas import tpu as pltpu
from jax.sharding import PartitionSpec as P

MESH = pl.DeviceIdType.MESH
EMPTY = -1e30
LANES = 128
ROWS = 8
SENT = 6
NY = 8


def kernel(
    seq, tensor, scale, ny, nz,
    owner_hbm, fill_hbm, q_hbm, cache_hbm, wuk_hbm, wuv_hbm, wout_hbm,
    out_ref,
    owner, fill, q_ref, qmine, qearly, qlate, cache, wuk, wuv, wout, bias, sel, pick, sendb, recvb, rf, xs, xr,
    joined_sem, local_sems, send1, recv1, send2, recv2, bsend, brecv, xsend, xrecv,
):
    pages, page, width = cache.shape
    heads, nope, latent = wuk.shape
    rope = width - latent
    tokens = pages * page
    columns = wout.shape[2]
    me = lax.axis_index("seq")
    tx = lax.axis_index("tensor")
    core = lax.rem(me, 2)
    y = lax.rem(lax.div(me, 2), ny)
    z = lax.div(me, 2 * ny)
    deep = nz // 2
    late = lax.div(z, deep)
    line = z * 2 + core
    block = lax.rem(line, 2 * deep) * ny
    half = seq // 2

    def along_y(k):
        return (z * ny + lax.rem(y + k, ny)) * 2 + core

    def in_half(part, k):
        at = part * 2 * deep + lax.rem(line + k, 2 * deep)
        return (lax.div(at, 2) * ny + y) * 2 + lax.rem(at, 2)

    small = [
        pltpu.make_async_copy(src, dst, local_sems.at[i])
        for i, (src, dst) in enumerate(((q_hbm, q_ref), (owner_hbm, owner), (fill_hbm, fill)))
    ]
    small[0].start()

    barrier = pltpu.get_barrier_semaphore()
    def tell(sem, peer):
        pl.semaphore_signal(sem, 1, device_id={"seq": peer}, device_id_type=MESH)

    def tell_half(sem, part, others_only):
        for k in range(2 * deep):
            peer = in_half(part, k)
            if others_only and k == 0:
                continue
            tell(sem, peer)

    for k in range(1, ny):
        tell(barrier, along_y(k))

    @pl.when(late == 0)
    def _():
        tell_half(barrier, 0, True)
        tell_half(barrier, 1, False)

    for k in range(1, tensor):
        pl.semaphore_signal(
            barrier, 1, device_id={"tensor": lax.rem(tx + k, tensor)}, device_id_type=MESH
        )

    small[1].start()
    small[2].start()

    small[0].wait()
    q = q_ref[...].astype(jnp.float32)
    step = nope + rope
    rows = [q[:, h * step : h * step + nope] for h in range(heads)]
    ropes = [q[:, h * step + nope : (h + 1) * step] for h in range(heads)]
    rows += [jnp.concatenate(ropes[h : h + 2], axis=1) for h in range(0, heads, 2)]
    rows += [jnp.zeros((ROWS - SENT, LANES), jnp.float32)]
    qmine[...] = jnp.concatenate(rows, axis=0).astype(jnp.bfloat16)[None]
    loads = [
        pltpu.make_async_copy(src, dst, local_sems.at[3 + i])
        for i, (src, dst) in enumerate(
            ((wuk_hbm, wuk), (cache_hbm, cache), (wuv_hbm, wuv))
            + tuple((wout_hbm.at[:, pl.ds(t * columns, columns)], wout.at[t]) for t in range(tensor))
        )
    ]
    queries = (qearly, qlate)
    sent = pl.ds(0, SENT)

    @pl.when(late == 0)
    def _():
        pl.semaphore_wait(barrier, ny - 1 + 2 * deep - 1 + tensor - 1)

    @pl.when(late == 1)
    def _():
        pl.semaphore_wait(barrier, ny - 1 + 2 * deep + tensor - 1)
        tell_half(joined_sem, 0, False)


    for part, buf in enumerate(queries):

        @pl.when(late == part)
        def _(buf=buf):
            mine = buf.at[pl.ds(block + y, 1), sent]
            for k in range(1, ny):
                pltpu.make_async_remote_copy(
                    src_ref=qmine.at[:, sent],
                    dst_ref=mine,
                    send_sem=send1,
                    recv_sem=recv1,
                    device_id={"seq": along_y(k)},
                    device_id_type=MESH,
                ).start()
            pltpu.make_async_copy(qmine.at[:, sent], mine, recv1).start()

    for load in loads:
        load.start()

    small[1].wait()
    small[2].wait()
    row16 = lax.broadcasted_iota(jnp.int32, (pages, LANES), 0)
    lane16 = lax.broadcasted_iota(jnp.int32, (pages, LANES), 1)
    own_row = jnp.zeros((pages, LANES), jnp.int32)
    own_lane = jnp.zeros((pages, LANES), jnp.int32)
    for p in range(pages):
        own_row = jnp.where(row16 == p, owner[p], own_row)
        own_lane = jnp.where((lane16 & (pages - 1)) == p, owner[p], own_lane)
    repeated = jnp.max(
        jnp.where((own_row == own_lane) & (row16 < (lane16 & (pages - 1))), 1, 0),
        axis=0, keepdims=True,
    )
    first_lane = jnp.where(repeated > 0, -1, own_lane[:1])
    big_row = lax.broadcasted_iota(jnp.int32, (seq * ROWS, LANES), 0)
    big_lane = lax.broadcasted_iota(jnp.int32, (seq * ROWS, LANES), 1)
    wanted = (first_lane * ROWS) + lax.div(big_lane[:1], pages)
    wanted = jnp.where((first_lane >= 0) & (big_lane[:1] < (heads + 1) * pages), wanted, -1)
    pick[...] = jnp.where(big_row == wanted, 1.0, 0.0).astype(jnp.bfloat16)
    own_rows = jnp.concatenate([own_row] * heads, axis=0)
    lane = lax.broadcasted_iota(jnp.int32, (1, LANES), 1)
    per = LANES // page
    for j in range(tokens // LANES):
        own_l = jnp.where(lane < page, owner[per * j], owner[per * j + 1])
        fill_l = jnp.where(lane < page, fill[per * j], fill[per * j + 1])
        own_l = jnp.where((lane & (page - 1)) < fill_l, own_l, -1)
        bias[:, j * LANES : (j + 1) * LANES] = jnp.where(own_rows == own_l, 0.0, EMPTY)

    def send_line(part, to):
        mine = queries[part].at[pl.ds(block, ny), sent]
        for k in range(1 if part == to else 0, 2 * deep):
            pltpu.make_async_remote_copy(
                src_ref=mine,
                dst_ref=mine,
                send_sem=send2,
                recv_sem=recv2.at[part],
                device_id={"seq": in_half(to, k)},
                device_id_type=MESH,
            ).start()

    for part, buf in enumerate(queries):

        @pl.when(late == part)
        def _(part=part, buf=buf):
            mine = buf.at[pl.ds(block, ny), sent]
            pltpu.make_async_copy(mine, mine, recv1).wait()
            send_line(part, 0)
            pl.semaphore_wait(joined_sem, 2 * deep)
            send_line(part, 1)
            if part == 0:
                tell_half(joined_sem, 1, False)

    for part, buf in enumerate(queries):
        for own, lines in ((part, 2 * deep - 1), (1 - part, 2 * deep)):

            @pl.when(late == own)
            def _(part=part, buf=buf, lines=lines):
                rest = buf.at[pl.ds(0, lines * ny), sent]
                pltpu.make_async_copy(rest, rest, recv2.at[part]).wait()

        for p in range(pages):
            spot = owner[p] & (half - 1)
            at = ((spot // (2 * ny)) * 2 + (spot & 1)) * ny + ((spot // 2) & (ny - 1))
            sel[p * ROWS : (p + 1) * ROWS, :] = buf[at].astype(jnp.float32)
        if part == 0:
            loads[0].wait()
        joined = []
        for h in range(heads):
            plain = sel[pl.ds(h, pages, stride=ROWS), :].astype(jnp.bfloat16)
            pair = sel[pl.ds(heads + h // 2, pages, stride=ROWS), :]
            turned = pair[:, (h % 2) * rope : (h % 2 + 1) * rope].astype(jnp.bfloat16)
            lat = jnp.dot(plain, wuk[h], preferred_element_type=jnp.float32)
            joined.append(jnp.concatenate([lat.astype(jnp.bfloat16), turned], axis=1))
        joined = jnp.concatenate(joined, axis=0)

        if part == 0:
            loads[1].wait()
        keys = cache[...].reshape(tokens, width)
        scores = lax.dot_general(
            joined, keys, (((1,), (1,)), ((), ())), preferred_element_type=jnp.float32
        )
        scores = scores * scale + bias[...]
        top = jnp.max(scores, axis=1, keepdims=True)
        top = jnp.where(top > 0.5 * EMPTY, top, 0.0)
        top_hi = top.astype(jnp.bfloat16).astype(jnp.float32)
        top_lo = (top - top_hi).astype(jnp.bfloat16).astype(jnp.float32)
        weights = jnp.exp(scores - (top_hi + top_lo))
        total = jnp.sum(weights, axis=1, keepdims=True)
        total_hi = total.astype(jnp.bfloat16).astype(jnp.float32)
        total_lo = total - total_hi
        sums = jnp.dot(
            weights.astype(jnp.bfloat16), keys[:, :latent], preferred_element_type=jnp.float32
        )

        if part == 0:
            loads[2].wait()
        blocks = [
            jnp.dot(
                sums[h * pages : (h + 1) * pages].astype(jnp.bfloat16), wuv[h],
                preferred_element_type=jnp.float32,
            )
            for h in range(heads)
        ]
        stats = jnp.zeros((pages, LANES), jnp.float32)
        for i, piece in enumerate((top_hi, top_lo, total_hi, total_lo)):
            for h in range(heads):
                stats = jnp.where(
                    lane16 == i * heads + h, piece[h * pages : (h + 1) * pages], stats
                )
        blocks += [stats, jnp.zeros((LANES - (heads + 1) * pages, LANES), jnp.float32)]
        table = jnp.concatenate(blocks, axis=0).astype(jnp.bfloat16)
        sendb[pl.ds(part * half, half)] = (
            jnp.dot(
                pick[pl.ds(part * half * ROWS, half * ROWS), :], table,
                preferred_element_type=jnp.float32,
            )
            .astype(jnp.bfloat16)
            .reshape(half, ROWS, LANES)
        )

        def send_sums(k, c, base):
            peer = base + lax.rem(me + k, 2 * ny)
            pltpu.make_async_remote_copy(
                src_ref=sendb.at[peer, sent],
                dst_ref=recvb.at[me, sent],
                send_sem=bsend,
                recv_sem=brecv,
                device_id={"seq": peer},
                device_id_type=MESH,
            ).start()
            return c

        for level in range(part * deep, (part + 1) * deep):
            lax.fori_loop(
                jnp.where(z == level, 1, 0), 2 * ny,
                functools.partial(send_sums, base=level * 2 * ny), 0,
            )

    recvb[me] = sendb[me]
    others = recvb.at[pl.ds(0, seq - 1), sent]
    pltpu.make_async_copy(others, others, brecv).wait()

    rf[...] = recvb[...].reshape(seq * ROWS, LANES).astype(jnp.float32)
    got = rf[pl.ds(heads, seq, stride=ROWS), :]
    tops = got + pltpu.roll(got, LANES - heads, 1)
    totals = pltpu.roll(got, LANES - 2 * heads, 1) + pltpu.roll(got, LANES - 3 * heads, 1)
    some = totals > 0.0
    tops = jnp.where(some, tops, EMPTY)
    peak = jnp.max(tops, axis=0, keepdims=True)
    share = jnp.where(some, jnp.exp(tops - peak), 0.0)
    denominator = jnp.sum(jnp.where(some, share * totals, 0.0), axis=0, keepdims=True)
    outs = []
    for h in range(heads):
        mine = rf[pl.ds(h, seq, stride=ROWS), :]
        numerator = jnp.sum(mine * share[:, h : h + 1], axis=0, keepdims=True)
        outs.append(numerator / denominator[:, h : h + 1])
    head_out = jnp.concatenate(outs, axis=1).astype(jnp.bfloat16)

    for load in loads[3:]:
        load.wait()
    sends = []
    for k in [2, 1, 3, 0]:
        peer = lax.rem(tx + k, tensor)
        piece = jnp.dot(head_out, wout[peer], preferred_element_type=jnp.float32)
        if k == 0:
            xr[tx] = piece
            continue
        xs[peer] = piece
        sends.append(
            pltpu.make_async_remote_copy(
                src_ref=xs.at[peer],
                dst_ref=xr.at[tx],
                send_sem=xsend.at[k],
                recv_sem=xrecv.at[k],
                device_id={"tensor": peer},
                device_id_type=MESH,
            )
        )
        sends[-1].start()
    for send in sends:
        send.wait_recv()
    total_value = xr[0]
    for t in range(1, tensor):
        total_value = total_value + xr[t]
    out_ref[...] = total_value.astype(out_ref.dtype)
    for send in sends:
        send.wait_send()
    away = qearly.at[pl.ds(0, ny - 1), sent]
    pltpu.make_async_copy(away, away, send1).wait()
    for _ in range(2 * nz - 1):
        away = qearly.at[pl.ds(0, ny), sent]
        pltpu.make_async_copy(away, away, send2).wait()
    away = sendb.at[pl.ds(0, seq - 1), sent]
    pltpu.make_async_copy(away, away, bsend).wait()


def solution(mesh):
    seq, tensor = mesh.shape["seq"], mesh.shape["tensor"]

    def shards(query, page_owner, page_fill, cache, w_uk, w_uv, w_out):
        heads = w_uk.shape[0]
        width = query.shape[1] // heads
        columns = w_out.shape[1] // tensor
        ny = NY

        def body(*refs):
            kernel(seq, tensor, 1.0 / math.sqrt(width), ny, seq // (2 * ny), *refs)

        vmem = pl.BlockSpec(memory_space=pltpu.VMEM)
        hbm = pl.BlockSpec(memory_space=pltpu.HBM)
        dma = pltpu.SemaphoreType.DMA
        return pl.pallas_call(
            body,
            out_shape=pltpu.VMEM((query.shape[0], columns), jnp.bfloat16),
            in_specs=[hbm] * 7,
            out_specs=vmem,
            scratch_shapes=[
                pltpu.SMEM(page_owner.shape, page_owner.dtype),
                pltpu.SMEM(page_fill.shape, page_fill.dtype),
                pltpu.VMEM(query.shape, query.dtype),
                pltpu.VMEM((1, ROWS, LANES), jnp.bfloat16),
                pltpu.VMEM((seq // 2, ROWS, LANES), jnp.bfloat16),
                pltpu.VMEM((seq // 2, ROWS, LANES), jnp.bfloat16),
                pltpu.VMEM(cache.shape, cache.dtype),
                pltpu.VMEM(w_uk.shape, w_uk.dtype),
                pltpu.VMEM(w_uv.shape, w_uv.dtype),
                pltpu.VMEM((tensor, w_out.shape[0], columns), w_out.dtype),
                pltpu.VMEM((page_owner.shape[0] * heads, cache.shape[0] * cache.shape[1]), jnp.float32),
                pltpu.VMEM((page_owner.shape[0] * ROWS, LANES), jnp.float32),
                pltpu.VMEM((seq * ROWS, LANES), jnp.bfloat16),
                pltpu.VMEM((seq, ROWS, LANES), jnp.bfloat16),
                pltpu.VMEM((seq, ROWS, LANES), jnp.bfloat16),
                pltpu.VMEM((seq * ROWS, LANES), jnp.float32),
                pltpu.VMEM((tensor, 1, columns), jnp.float32),
                pltpu.VMEM((tensor, 1, columns), jnp.float32),
                pltpu.SemaphoreType.REGULAR,
                dma((10,)),
                dma, dma, dma,
                dma((2,)),
                dma, dma,
                dma((tensor,)),
                dma((tensor,)),
            ],
            compiler_params=pltpu.CompilerParams(collective_id=0, has_side_effects=True),
        )(page_owner, page_fill, query, cache, w_uk, w_uv, w_out)

    return jax.shard_map(
        shards,
        mesh=mesh,
        in_specs=(
            P("seq", "tensor"), P("seq"), P("seq"), P("seq", None, None),
            P("tensor", None, None), P("tensor", None, None), P("tensor", None),
        ),
        out_specs=P("seq", "tensor"),
        check_vma=False,
    )
```

```python
import functools
import math

import jax
import jax.numpy as jnp
from jax import lax
from jax.experimental import pallas as pl
from jax.experimental.pallas import tpu as pltpu
from jax.sharding import PartitionSpec as P

MESH = pl.DeviceIdType.MESH
EMPTY = -1e30
LANES = 128
ROWS = 8
SENT = 6
NY = 8


def kernel(
    seq, tensor, scale, ny, nz,
    owner_hbm, fill_hbm, q_hbm, cache_hbm, wuk_hbm, wuv_hbm, wout_hbm,
    out_ref,
    owner, fill, q_ref, qmine, qearly, qlate, cache, wuk, wuv, wout, bias, sel, pick, sendb, recvb, rf, xs, xr,
    chip_in, line_in, local_sems, send1, recv1, send2, recv2, bsend, brecv, xsend, xrecv,
):
    pages, page, width = cache.shape
    heads, nope, latent = wuk.shape
    rope = width - latent
    tokens = pages * page
    columns = wout.shape[2]
    me = lax.axis_index("seq")
    tx = lax.axis_index("tensor")
    core = lax.rem(me, 2)
    y = lax.rem(lax.div(me, 2), ny)
    z = lax.div(me, 2 * ny)
    deep = nz // 2
    late = lax.div(z, deep)
    line = z * 2 + core
    block = lax.rem(line, 2 * deep) * ny
    half = seq // 2

    def along_y(k):
        return (z * ny + lax.rem(y + k, ny)) * 2 + core

    def in_half(part, k):
        at = part * 2 * deep + lax.rem(line + k, 2 * deep)
        return (lax.div(at, 2) * ny + y) * 2 + lax.rem(at, 2)

    small = [
        pltpu.make_async_copy(src, dst, local_sems.at[i])
        for i, (src, dst) in enumerate(((q_hbm, q_ref), (owner_hbm, owner), (fill_hbm, fill)))
    ]
    small[0].start()

    barrier = pltpu.get_barrier_semaphore()

    def tell(sem, peer):
        pl.semaphore_signal(sem, 1, device_id={"seq": peer}, device_id_type=MESH)

    def tell_half(sem, part, others_only):
        for k in range(2 * deep):
            peer = in_half(part, k)
            if others_only and k == 0:
                continue
            tell(sem, peer)

    def tell_tensor(seat):
        for k in range(1, tensor):
            pl.semaphore_signal(
                barrier, 1,
                device_id={"seq": seat, "tensor": lax.rem(tx + k, tensor)},
                device_id_type=MESH,
            )

    first_core, sibling = me - core, me + 1 - 2 * core

    @pl.when(late == 0)
    def _():
        for k in range(1, ny):
            tell(barrier, along_y(k))
        tell_half(barrier, 0, True)
        for k in range(deep):
            tell(barrier, (deep + lax.rem(z + k, deep)) * 2 * ny + y * 2)
        tell_tensor(me)

    @pl.when(late == 1)
    def _():
        tell(barrier, sibling)
        for k in range(1, ny):
            tell(barrier, along_y(k) + 1 - core)
        tell_tensor(first_core + 1)

    small[1].start()
    small[2].start()

    @pl.when((late == 1) & (core == 0))
    def _():
        pl.semaphore_wait(barrier, 2 * deep + 1)
        for k in range(2 * deep):
            tell(chip_in.at[z - deep], in_half(0, k))
        tell(line_in.at[0], sibling)

    small[0].wait()
    q = q_ref[...].astype(jnp.float32)
    step = nope + rope
    rows = [q[:, h * step : h * step + nope] for h in range(heads)]
    ropes = [q[:, h * step + nope : (h + 1) * step] for h in range(heads)]
    rows += [jnp.concatenate(ropes[h : h + 2], axis=1) for h in range(0, heads, 2)]
    rows += [jnp.zeros((ROWS - SENT, LANES), jnp.float32)]
    qmine[...] = jnp.concatenate(rows, axis=0).astype(jnp.bfloat16)[None]
    loads = [
        pltpu.make_async_copy(src, dst, local_sems.at[3 + i])
        for i, (src, dst) in enumerate(
            ((wuk_hbm, wuk), (cache_hbm, cache), (wuv_hbm, wuv))
            + tuple((wout_hbm.at[:, pl.ds(t * columns, columns)], wout.at[t]) for t in range(tensor))
        )
    ]
    queries = (qearly, qlate)
    sent = pl.ds(0, SENT)

    @pl.when(late == 0)
    def _():
        pl.semaphore_wait(barrier, ny - 1 + 2 * deep - 1 + tensor - 1)

    @pl.when((late == 1) & (core == 1))
    def _():
        pl.semaphore_wait(barrier, 2 * (ny - 1) + 2 * (tensor - 1) + 1)
        tell(line_in.at[0], sibling)

    @pl.when(late == 1)
    def _():
        pl.semaphore_wait(line_in.at[0], 1)

    for part, buf in enumerate(queries):

        @pl.when(late == part)
        def _(buf=buf):
            mine = buf.at[pl.ds(block + y, 1), sent]
            for k in range(1, ny):
                pltpu.make_async_remote_copy(
                    src_ref=qmine.at[:, sent],
                    dst_ref=mine,
                    send_sem=send1,
                    recv_sem=recv1,
                    device_id={"seq": along_y(k)},
                    device_id_type=MESH,
                ).start()
            pltpu.make_async_copy(qmine.at[:, sent], mine, recv1).start()

    for load in loads:
        load.start()

    small[1].wait()
    small[2].wait()
    row16 = lax.broadcasted_iota(jnp.int32, (pages, LANES), 0)
    lane16 = lax.broadcasted_iota(jnp.int32, (pages, LANES), 1)
    own_row = jnp.zeros((pages, LANES), jnp.int32)
    own_lane = jnp.zeros((pages, LANES), jnp.int32)
    for p in range(pages):
        own_row = jnp.where(row16 == p, owner[p], own_row)
        own_lane = jnp.where((lane16 & (pages - 1)) == p, owner[p], own_lane)
    repeated = jnp.max(
        jnp.where((own_row == own_lane) & (row16 < (lane16 & (pages - 1))), 1, 0),
        axis=0, keepdims=True,
    )
    first_lane = jnp.where(repeated > 0, -1, own_lane[:1])
    big_row = lax.broadcasted_iota(jnp.int32, (seq * ROWS, LANES), 0)
    big_lane = lax.broadcasted_iota(jnp.int32, (seq * ROWS, LANES), 1)
    wanted = (first_lane * ROWS) + lax.div(big_lane[:1], pages)
    wanted = jnp.where((first_lane >= 0) & (big_lane[:1] < (heads + 1) * pages), wanted, -1)
    pick[...] = jnp.where(big_row == wanted, 1.0, 0.0).astype(jnp.bfloat16)
    own_rows = jnp.concatenate([own_row] * heads, axis=0)
    lane = lax.broadcasted_iota(jnp.int32, (1, LANES), 1)
    per = LANES // page
    for j in range(tokens // LANES):
        own_l = jnp.where(lane < page, owner[per * j], owner[per * j + 1])
        fill_l = jnp.where(lane < page, fill[per * j], fill[per * j + 1])
        own_l = jnp.where((lane & (page - 1)) < fill_l, own_l, -1)
        bias[:, j * LANES : (j + 1) * LANES] = jnp.where(own_rows == own_l, 0.0, EMPTY)

    def send_line(part, peers):
        mine = queries[part].at[pl.ds(block, ny), sent]
        for peer in peers:
            pltpu.make_async_remote_copy(
                src_ref=mine,
                dst_ref=mine,
                send_sem=send2,
                recv_sem=recv2.at[part],
                device_id={"seq": peer},
                device_id_type=MESH,
            ).start()

    for part, buf in enumerate(queries):

        @pl.when(late == part)
        def _(part=part, buf=buf):
            mine = buf.at[pl.ds(block, ny), sent]
            pltpu.make_async_copy(mine, mine, recv1).wait()
            if part == 0:
                send_line(0, [in_half(0, k) for k in range(1, 2 * deep)])
                for j in range(deep):
                    pl.semaphore_wait(chip_in.at[j], 1)
                    send_line(0, [((deep + j) * ny + y) * 2 + c for c in range(2)])
                for k in range(2 * deep):
                    tell(line_in.at[1], in_half(1, k))
            else:
                send_line(1, [in_half(0, k) for k in range(2 * deep)])
                pl.semaphore_wait(line_in.at[1], 2 * deep)
                send_line(1, [in_half(1, k) for k in range(1, 2 * deep)])

    for part, buf in enumerate(queries):
        for own, lines in ((part, 2 * deep - 1), (1 - part, 2 * deep)):

            @pl.when(late == own)
            def _(part=part, buf=buf, lines=lines):
                rest = buf.at[pl.ds(0, lines * ny), sent]
                pltpu.make_async_copy(rest, rest, recv2.at[part]).wait()

        for p in range(pages):
            spot = owner[p] & (half - 1)
            at = ((spot // (2 * ny)) * 2 + (spot & 1)) * ny + ((spot // 2) & (ny - 1))
            sel[p * ROWS : (p + 1) * ROWS, :] = buf[at].astype(jnp.float32)
        if part == 0:
            loads[0].wait()
        joined = []
        for h in range(heads):
            plain = sel[pl.ds(h, pages, stride=ROWS), :].astype(jnp.bfloat16)
            pair = sel[pl.ds(heads + h // 2, pages, stride=ROWS), :]
            turned = pair[:, (h % 2) * rope : (h % 2 + 1) * rope].astype(jnp.bfloat16)
            lat = jnp.dot(plain, wuk[h], preferred_element_type=jnp.float32)
            joined.append(jnp.concatenate([lat.astype(jnp.bfloat16), turned], axis=1))
        joined = jnp.concatenate(joined, axis=0)

        if part == 0:
            loads[1].wait()
        keys = cache[...].reshape(tokens, width)
        scores = lax.dot_general(
            joined, keys, (((1,), (1,)), ((), ())), preferred_element_type=jnp.float32
        )
        scores = scores * scale + bias[...]
        top = jnp.max(scores, axis=1, keepdims=True)
        top = jnp.where(top > 0.5 * EMPTY, top, 0.0)
        top_hi = top.astype(jnp.bfloat16).astype(jnp.float32)
        top_lo = (top - top_hi).astype(jnp.bfloat16).astype(jnp.float32)
        weights = jnp.exp(scores - (top_hi + top_lo))
        total = jnp.sum(weights, axis=1, keepdims=True)
        total_hi = total.astype(jnp.bfloat16).astype(jnp.float32)
        total_lo = total - total_hi
        sums = jnp.dot(
            weights.astype(jnp.bfloat16), keys[:, :latent], preferred_element_type=jnp.float32
        )

        if part == 0:
            loads[2].wait()
        blocks = [
            jnp.dot(
                sums[h * pages : (h + 1) * pages].astype(jnp.bfloat16), wuv[h],
                preferred_element_type=jnp.float32,
            )
            for h in range(heads)
        ]
        stats = jnp.zeros((pages, LANES), jnp.float32)
        for i, piece in enumerate((top_hi, top_lo, total_hi, total_lo)):
            for h in range(heads):
                stats = jnp.where(
                    lane16 == i * heads + h, piece[h * pages : (h + 1) * pages], stats
                )
        blocks += [stats, jnp.zeros((LANES - (heads + 1) * pages, LANES), jnp.float32)]
        table = jnp.concatenate(blocks, axis=0).astype(jnp.bfloat16)
        sendb[pl.ds(part * half, half)] = (
            jnp.dot(
                pick[pl.ds(part * half * ROWS, half * ROWS), :], table,
                preferred_element_type=jnp.float32,
            )
            .astype(jnp.bfloat16)
            .reshape(half, ROWS, LANES)
        )

        def send_sums(k, c, base):
            peer = base + lax.rem(me + k, 2 * ny)
            pltpu.make_async_remote_copy(
                src_ref=sendb.at[peer, sent],
                dst_ref=recvb.at[me, sent],
                send_sem=bsend,
                recv_sem=brecv,
                device_id={"seq": peer},
                device_id_type=MESH,
            ).start()
            return c

        for level in range(part * deep, (part + 1) * deep):
            lax.fori_loop(
                jnp.where(z == level, 1, 0), 2 * ny,
                functools.partial(send_sums, base=level * 2 * ny), 0,
            )

    recvb[me] = sendb[me]
    others = recvb.at[pl.ds(0, seq - 1), sent]
    pltpu.make_async_copy(others, others, brecv).wait()

    rf[...] = recvb[...].reshape(seq * ROWS, LANES).astype(jnp.float32)
    got = rf[pl.ds(heads, seq, stride=ROWS), :]
    tops = got + pltpu.roll(got, LANES - heads, 1)
    totals = pltpu.roll(got, LANES - 2 * heads, 1) + pltpu.roll(got, LANES - 3 * heads, 1)
    some = totals > 0.0
    tops = jnp.where(some, tops, EMPTY)
    peak = jnp.max(tops, axis=0, keepdims=True)
    share = jnp.where(some, jnp.exp(tops - peak), 0.0)
    denominator = jnp.sum(jnp.where(some, share * totals, 0.0), axis=0, keepdims=True)
    outs = []
    for h in range(heads):
        mine = rf[pl.ds(h, seq, stride=ROWS), :]
        numerator = jnp.sum(mine * share[:, h : h + 1], axis=0, keepdims=True)
        outs.append(numerator / denominator[:, h : h + 1])
    head_out = jnp.concatenate(outs, axis=1).astype(jnp.bfloat16)

    for load in loads[3:]:
        load.wait()
    sends = []
    for k in [2, 1, 3, 0]:
        peer = lax.rem(tx + k, tensor)
        piece = jnp.dot(head_out, wout[peer], preferred_element_type=jnp.float32)
        if k == 0:
            xr[tx] = piece
            continue
        xs[peer] = piece
        sends.append(
            pltpu.make_async_remote_copy(
                src_ref=xs.at[peer],
                dst_ref=xr.at[tx],
                send_sem=xsend.at[k],
                recv_sem=xrecv.at[k],
                device_id={"tensor": peer},
                device_id_type=MESH,
            )
        )
        sends[-1].start()
    for send in sends:
        send.wait_recv()
    total_value = xr[0]
    for t in range(1, tensor):
        total_value = total_value + xr[t]
    out_ref[...] = total_value.astype(out_ref.dtype)
    for send in sends:
        send.wait_send()
    away = qearly.at[pl.ds(0, ny - 1), sent]
    pltpu.make_async_copy(away, away, send1).wait()
    for _ in range(2 * nz - 1):
        away = qearly.at[pl.ds(0, ny), sent]
        pltpu.make_async_copy(away, away, send2).wait()
    away = sendb.at[pl.ds(0, seq - 1), sent]
    pltpu.make_async_copy(away, away, bsend).wait()


def solution(mesh):
    seq, tensor = mesh.shape["seq"], mesh.shape["tensor"]

    def shards(query, page_owner, page_fill, cache, w_uk, w_uv, w_out):
        heads = w_uk.shape[0]
        width = query.shape[1] // heads
        columns = w_out.shape[1] // tensor
        ny = NY

        def body(*refs):
            kernel(seq, tensor, 1.0 / math.sqrt(width), ny, seq // (2 * ny), *refs)

        vmem = pl.BlockSpec(memory_space=pltpu.VMEM)
        hbm = pl.BlockSpec(memory_space=pltpu.HBM)
        dma = pltpu.SemaphoreType.DMA
        return pl.pallas_call(
            body,
            out_shape=pltpu.VMEM((query.shape[0], columns), jnp.bfloat16),
            in_specs=[hbm] * 7,
            out_specs=vmem,
            scratch_shapes=[
                pltpu.SMEM(page_owner.shape, page_owner.dtype),
                pltpu.SMEM(page_fill.shape, page_fill.dtype),
                pltpu.VMEM(query.shape, query.dtype),
                pltpu.VMEM((1, ROWS, LANES), jnp.bfloat16),
                pltpu.VMEM((seq // 2, ROWS, LANES), jnp.bfloat16),
                pltpu.VMEM((seq // 2, ROWS, LANES), jnp.bfloat16),
                pltpu.VMEM(cache.shape, cache.dtype),
                pltpu.VMEM(w_uk.shape, w_uk.dtype),
                pltpu.VMEM(w_uv.shape, w_uv.dtype),
                pltpu.VMEM((tensor, w_out.shape[0], columns), w_out.dtype),
                pltpu.VMEM((page_owner.shape[0] * heads, cache.shape[0] * cache.shape[1]), jnp.float32),
                pltpu.VMEM((page_owner.shape[0] * ROWS, LANES), jnp.float32),
                pltpu.VMEM((seq * ROWS, LANES), jnp.bfloat16),
                pltpu.VMEM((seq, ROWS, LANES), jnp.bfloat16),
                pltpu.VMEM((seq, ROWS, LANES), jnp.bfloat16),
                pltpu.VMEM((seq * ROWS, LANES), jnp.float32),
                pltpu.VMEM((tensor, 1, columns), jnp.float32),
                pltpu.VMEM((tensor, 1, columns), jnp.float32),
                pltpu.SemaphoreType.REGULAR((seq // (4 * ny),)),
                pltpu.SemaphoreType.REGULAR((2,)),
                dma((10,)),
                dma, dma, dma,
                dma((2,)),
                dma, dma,
                dma((tensor,)),
                dma((tensor,)),
            ],
            compiler_params=pltpu.CompilerParams(collective_id=0, has_side_effects=True),
        )(page_owner, page_fill, query, cache, w_uk, w_uv, w_out)

    return jax.shard_map(
        shards,
        mesh=mesh,
        in_specs=(
            P("seq", "tensor"), P("seq"), P("seq"), P("seq", None, None),
            P("tensor", None, None), P("tensor", None, None), P("tensor", None),
        ),
        out_specs=P("seq", "tensor"),
        check_vma=False,
    )
```

```python
import functools
import math

import jax
import jax.numpy as jnp
from jax import lax
from jax.experimental import pallas as pl
from jax.experimental.pallas import tpu as pltpu
from jax.sharding import PartitionSpec as P

MESH = pl.DeviceIdType.MESH
EMPTY = -1e30
LANES = 128
ROWS = 8
SENT = 6
NY = 8


def kernel(
    seq, tensor, scale, ny, nz,
    owner_hbm, fill_hbm, q_hbm, cache_hbm, wuk_hbm, wuv_hbm, wout_hbm,
    out_ref,
    owner, fill, q_ref, qmine, qearly, qlate, cache, wuk, wuv, wout, bias, sel, pick, sendb, recvb, rf, xs, xr,
    chip_in, line_in, local_sems, send1, recv1, send2, recv2, send3, recv3, bsend, brecv, xsend, xrecv,
):
    pages, page, width = cache.shape
    heads, nope, latent = wuk.shape
    rope = width - latent
    tokens = pages * page
    columns = wout.shape[2]
    me = lax.axis_index("seq")
    tx = lax.axis_index("tensor")
    core = lax.rem(me, 2)
    y = lax.rem(lax.div(me, 2), ny)
    z = lax.div(me, 2 * ny)
    deep = nz // 2
    late = lax.div(z, deep)
    line = z * 2 + core
    near = core * deep * ny
    block = near + lax.rem(z, deep) * ny
    half = seq // 2

    def along_y(k):
        return (z * ny + lax.rem(y + k, ny)) * 2 + core

    def in_half(part, k):
        at = part * 2 * deep + lax.rem(line + k, 2 * deep)
        return (lax.div(at, 2) * ny + y) * 2 + lax.rem(at, 2)

    small = [
        pltpu.make_async_copy(src, dst, local_sems.at[i])
        for i, (src, dst) in enumerate(((q_hbm, q_ref), (owner_hbm, owner), (fill_hbm, fill)))
    ]
    small[0].start()

    barrier = pltpu.get_barrier_semaphore()

    def tell(sem, peer):
        pl.semaphore_signal(sem, 1, device_id={"seq": peer}, device_id_type=MESH)

    def tell_half(sem, part, others_only):
        for k in range(2 * deep):
            peer = in_half(part, k)
            if others_only and k == 0:
                continue
            tell(sem, peer)

    def like_core(part, k):
        return ((part * deep + lax.rem(z + k, deep)) * ny + y) * 2 + core

    def tell_tensor(seat):
        for k in range(1, tensor):
            pl.semaphore_signal(
                barrier, 1,
                device_id={"seq": seat, "tensor": lax.rem(tx + k, tensor)},
                device_id_type=MESH,
            )

    first_core, sibling = me - core, me + 1 - 2 * core

    @pl.when(late == 0)
    def _():
        for k in range(1, ny):
            tell(barrier, along_y(k))
        tell_half(barrier, 0, True)
        for k in range(deep):
            tell(barrier, (deep + lax.rem(z + k, deep)) * 2 * ny + y * 2)
        tell_tensor(me)

    @pl.when(late == 1)
    def _():
        tell(barrier, sibling)
        for k in range(1, ny):
            tell(barrier, along_y(k) + 1 - core)
        tell_tensor(first_core + 1)

    small[1].start()
    small[2].start()

    @pl.when((late == 1) & (core == 0))
    def _():
        pl.semaphore_wait(barrier, 2 * deep + 1)
        for k in range(2 * deep):
            tell(chip_in.at[z - deep], in_half(0, k))
        tell(line_in.at[0], sibling)

    small[0].wait()
    q = q_ref[...].astype(jnp.float32)
    step = nope + rope
    rows = [q[:, h * step : h * step + nope] for h in range(heads)]
    ropes = [q[:, h * step + nope : (h + 1) * step] for h in range(heads)]
    rows += [jnp.concatenate(ropes[h : h + 2], axis=1) for h in range(0, heads, 2)]
    rows += [jnp.zeros((ROWS - SENT, LANES), jnp.float32)]
    qmine[...] = jnp.concatenate(rows, axis=0).astype(jnp.bfloat16)[None]
    loads = [
        pltpu.make_async_copy(src, dst, local_sems.at[3 + i])
        for i, (src, dst) in enumerate(
            ((wuk_hbm, wuk), (cache_hbm, cache), (wuv_hbm, wuv))
            + tuple((wout_hbm.at[:, pl.ds(t * columns, columns)], wout.at[t]) for t in range(tensor))
        )
    ]
    queries = (qearly, qlate)
    sent = pl.ds(0, SENT)

    @pl.when(late == 0)
    def _():
        pl.semaphore_wait(barrier, ny - 1 + 2 * deep - 1 + tensor - 1)

    @pl.when((late == 1) & (core == 1))
    def _():
        pl.semaphore_wait(barrier, 2 * (ny - 1) + 2 * (tensor - 1) + 1)
        tell(line_in.at[0], sibling)

    @pl.when(late == 1)
    def _():
        pl.semaphore_wait(line_in.at[0], 1)

    for part, buf in enumerate(queries):

        @pl.when(late == part)
        def _(buf=buf):
            mine = buf.at[pl.ds(block + y, 1), sent]
            for k in range(1, ny):
                pltpu.make_async_remote_copy(
                    src_ref=qmine.at[:, sent],
                    dst_ref=mine,
                    send_sem=send1,
                    recv_sem=recv1,
                    device_id={"seq": along_y(k)},
                    device_id_type=MESH,
                ).start()
            pltpu.make_async_copy(qmine.at[:, sent], mine, recv1).start()

    for load in loads:
        load.start()

    small[1].wait()
    small[2].wait()
    row16 = lax.broadcasted_iota(jnp.int32, (pages, LANES), 0)
    lane16 = lax.broadcasted_iota(jnp.int32, (pages, LANES), 1)
    own_row = jnp.zeros((pages, LANES), jnp.int32)
    own_lane = jnp.zeros((pages, LANES), jnp.int32)
    for p in range(pages):
        own_row = jnp.where(row16 == p, owner[p], own_row)
        own_lane = jnp.where((lane16 & (pages - 1)) == p, owner[p], own_lane)
    repeated = jnp.max(
        jnp.where((own_row == own_lane) & (row16 < (lane16 & (pages - 1))), 1, 0),
        axis=0, keepdims=True,
    )
    first_lane = jnp.where(repeated > 0, -1, own_lane[:1])
    big_row = lax.broadcasted_iota(jnp.int32, (seq * ROWS, LANES), 0)
    big_lane = lax.broadcasted_iota(jnp.int32, (seq * ROWS, LANES), 1)
    wanted = (first_lane * ROWS) + lax.div(big_lane[:1], pages)
    wanted = jnp.where((first_lane >= 0) & (big_lane[:1] < (heads + 1) * pages), wanted, -1)
    pick[...] = jnp.where(big_row == wanted, 1.0, 0.0).astype(jnp.bfloat16)
    own_rows = jnp.concatenate([own_row] * heads, axis=0)
    lane = lax.broadcasted_iota(jnp.int32, (1, LANES), 1)
    per = LANES // page
    for j in range(tokens // LANES):
        own_l = jnp.where(lane < page, owner[per * j], owner[per * j + 1])
        fill_l = jnp.where(lane < page, fill[per * j], fill[per * j + 1])
        own_l = jnp.where((lane & (page - 1)) < fill_l, own_l, -1)
        bias[:, j * LANES : (j + 1) * LANES] = jnp.where(own_rows == own_l, 0.0, EMPTY)

    def send_line(part, peers):
        mine = queries[part].at[pl.ds(block, ny), sent]
        for peer in peers:
            pltpu.make_async_remote_copy(
                src_ref=mine,
                dst_ref=mine,
                send_sem=send2,
                recv_sem=recv2.at[part],
                device_id={"seq": peer},
                device_id_type=MESH,
            ).start()

    for part, buf in enumerate(queries):

        @pl.when(late == part)
        def _(part=part, buf=buf):
            mine = buf.at[pl.ds(block, ny), sent]
            pltpu.make_async_copy(mine, mine, recv1).wait()
            if part == 0:
                send_line(0, [like_core(0, k) for k in range(1, deep)])
                for j in range(deep):
                    pl.semaphore_wait(chip_in.at[j], 1)
                    send_line(0, [((deep + j) * ny + y) * 2 + core])
                for k in range(2 * deep):
                    tell(line_in.at[1], in_half(1, k))
            else:
                send_line(1, [like_core(0, k) for k in range(deep)])
                pl.semaphore_wait(line_in.at[1], 2 * deep)
                send_line(1, [like_core(1, k) for k in range(1, deep)])

    swaps = []
    for part, buf in enumerate(queries):
        for own, lines in ((part, deep - 1), (1 - part, deep)):

            @pl.when(late == own)
            def _(part=part, buf=buf, lines=lines):
                rest = buf.at[pl.ds(0, lines * ny), sent]
                pltpu.make_async_copy(rest, rest, recv2.at[part]).wait()

        heard = buf.at[pl.ds(near, deep * ny), sent]
        swap = pltpu.make_async_remote_copy(
            src_ref=heard,
            dst_ref=heard,
            send_sem=send3.at[part],
            recv_sem=recv3.at[part],
            device_id={"seq": sibling},
            device_id_type=MESH,
        )
        swap.start()
        swaps.append(swap)
        swap.wait_recv()

        for p in range(pages):
            spot = owner[p] & (half - 1)
            at = ((spot & 1) * deep + spot // (2 * ny)) * ny + ((spot // 2) & (ny - 1))
            sel[p * ROWS : (p + 1) * ROWS, :] = buf[at].astype(jnp.float32)
        if part == 0:
            loads[0].wait()
        joined = []
        for h in range(heads):
            plain = sel[pl.ds(h, pages, stride=ROWS), :].astype(jnp.bfloat16)
            pair = sel[pl.ds(heads + h // 2, pages, stride=ROWS), :]
            turned = pair[:, (h % 2) * rope : (h % 2 + 1) * rope].astype(jnp.bfloat16)
            lat = jnp.dot(plain, wuk[h], preferred_element_type=jnp.float32)
            joined.append(jnp.concatenate([lat.astype(jnp.bfloat16), turned], axis=1))
        joined = jnp.concatenate(joined, axis=0)

        if part == 0:
            loads[1].wait()
        keys = cache[...].reshape(tokens, width)
        scores = lax.dot_general(
            joined, keys, (((1,), (1,)), ((), ())), preferred_element_type=jnp.float32
        )
        scores = scores * scale + bias[...]
        top = jnp.max(scores, axis=1, keepdims=True)
        top = jnp.where(top > 0.5 * EMPTY, top, 0.0)
        top_hi = top.astype(jnp.bfloat16).astype(jnp.float32)
        top_lo = (top - top_hi).astype(jnp.bfloat16).astype(jnp.float32)
        weights = jnp.exp(scores - (top_hi + top_lo))
        total = jnp.sum(weights, axis=1, keepdims=True)
        total_hi = total.astype(jnp.bfloat16).astype(jnp.float32)
        total_lo = total - total_hi
        sums = jnp.dot(
            weights.astype(jnp.bfloat16), keys[:, :latent], preferred_element_type=jnp.float32
        )

        if part == 0:
            loads[2].wait()
        blocks = [
            jnp.dot(
                sums[h * pages : (h + 1) * pages].astype(jnp.bfloat16), wuv[h],
                preferred_element_type=jnp.float32,
            )
            for h in range(heads)
        ]
        stats = jnp.zeros((pages, LANES), jnp.float32)
        for i, piece in enumerate((top_hi, top_lo, total_hi, total_lo)):
            for h in range(heads):
                stats = jnp.where(
                    lane16 == i * heads + h, piece[h * pages : (h + 1) * pages], stats
                )
        blocks += [stats, jnp.zeros((LANES - (heads + 1) * pages, LANES), jnp.float32)]
        table = jnp.concatenate(blocks, axis=0).astype(jnp.bfloat16)
        sendb[pl.ds(part * half, half)] = (
            jnp.dot(
                pick[pl.ds(part * half * ROWS, half * ROWS), :], table,
                preferred_element_type=jnp.float32,
            )
            .astype(jnp.bfloat16)
            .reshape(half, ROWS, LANES)
        )

        def send_sums(k, c, base):
            peer = base + lax.rem(me + k, 2 * ny)
            pltpu.make_async_remote_copy(
                src_ref=sendb.at[peer, sent],
                dst_ref=recvb.at[me, sent],
                send_sem=bsend,
                recv_sem=brecv,
                device_id={"seq": peer},
                device_id_type=MESH,
            ).start()
            return c

        for level in range(part * deep, (part + 1) * deep):
            lax.fori_loop(
                jnp.where(z == level, 1, 0), 2 * ny,
                functools.partial(send_sums, base=level * 2 * ny), 0,
            )

    recvb[me] = sendb[me]
    others = recvb.at[pl.ds(0, seq - 1), sent]
    pltpu.make_async_copy(others, others, brecv).wait()

    rf[...] = recvb[...].reshape(seq * ROWS, LANES).astype(jnp.float32)
    got = rf[pl.ds(heads, seq, stride=ROWS), :]
    tops = got + pltpu.roll(got, LANES - heads, 1)
    totals = pltpu.roll(got, LANES - 2 * heads, 1) + pltpu.roll(got, LANES - 3 * heads, 1)
    some = totals > 0.0
    tops = jnp.where(some, tops, EMPTY)
    peak = jnp.max(tops, axis=0, keepdims=True)
    share = jnp.where(some, jnp.exp(tops - peak), 0.0)
    denominator = jnp.sum(jnp.where(some, share * totals, 0.0), axis=0, keepdims=True)
    outs = []
    for h in range(heads):
        mine = rf[pl.ds(h, seq, stride=ROWS), :]
        numerator = jnp.sum(mine * share[:, h : h + 1], axis=0, keepdims=True)
        outs.append(numerator / denominator[:, h : h + 1])
    head_out = jnp.concatenate(outs, axis=1).astype(jnp.bfloat16)

    for load in loads[3:]:
        load.wait()
    sends = []
    for k in [2, 1, 3, 0]:
        peer = lax.rem(tx + k, tensor)
        piece = jnp.dot(head_out, wout[peer], preferred_element_type=jnp.float32)
        if k == 0:
            xr[tx] = piece
            continue
        xs[peer] = piece
        sends.append(
            pltpu.make_async_remote_copy(
                src_ref=xs.at[peer],
                dst_ref=xr.at[tx],
                send_sem=xsend.at[k],
                recv_sem=xrecv.at[k],
                device_id={"tensor": peer},
                device_id_type=MESH,
            )
        )
        sends[-1].start()
    for send in sends:
        send.wait_recv()
    total_value = xr[0]
    for t in range(1, tensor):
        total_value = total_value + xr[t]
    out_ref[...] = total_value.astype(out_ref.dtype)
    for send in sends:
        send.wait_send()
    away = qearly.at[pl.ds(0, ny - 1), sent]
    pltpu.make_async_copy(away, away, send1).wait()
    away = qearly.at[pl.ds(0, (nz - 1) * ny), sent]
    pltpu.make_async_copy(away, away, send2).wait()
    for swap in swaps:
        swap.wait_send()
    away = sendb.at[pl.ds(0, seq - 1), sent]
    pltpu.make_async_copy(away, away, bsend).wait()


def solution(mesh):
    seq, tensor = mesh.shape["seq"], mesh.shape["tensor"]

    def shards(query, page_owner, page_fill, cache, w_uk, w_uv, w_out):
        heads = w_uk.shape[0]
        width = query.shape[1] // heads
        columns = w_out.shape[1] // tensor
        ny = NY

        def body(*refs):
            kernel(seq, tensor, 1.0 / math.sqrt(width), ny, seq // (2 * ny), *refs)

        vmem = pl.BlockSpec(memory_space=pltpu.VMEM)
        hbm = pl.BlockSpec(memory_space=pltpu.HBM)
        dma = pltpu.SemaphoreType.DMA
        return pl.pallas_call(
            body,
            out_shape=pltpu.VMEM((query.shape[0], columns), jnp.bfloat16),
            in_specs=[hbm] * 7,
            out_specs=vmem,
            scratch_shapes=[
                pltpu.SMEM(page_owner.shape, page_owner.dtype),
                pltpu.SMEM(page_fill.shape, page_fill.dtype),
                pltpu.VMEM(query.shape, query.dtype),
                pltpu.VMEM((1, ROWS, LANES), jnp.bfloat16),
                pltpu.VMEM((seq // 2, ROWS, LANES), jnp.bfloat16),
                pltpu.VMEM((seq // 2, ROWS, LANES), jnp.bfloat16),
                pltpu.VMEM(cache.shape, cache.dtype),
                pltpu.VMEM(w_uk.shape, w_uk.dtype),
                pltpu.VMEM(w_uv.shape, w_uv.dtype),
                pltpu.VMEM((tensor, w_out.shape[0], columns), w_out.dtype),
                pltpu.VMEM((page_owner.shape[0] * heads, cache.shape[0] * cache.shape[1]), jnp.float32),
                pltpu.VMEM((page_owner.shape[0] * ROWS, LANES), jnp.float32),
                pltpu.VMEM((seq * ROWS, LANES), jnp.bfloat16),
                pltpu.VMEM((seq, ROWS, LANES), jnp.bfloat16),
                pltpu.VMEM((seq, ROWS, LANES), jnp.bfloat16),
                pltpu.VMEM((seq * ROWS, LANES), jnp.float32),
                pltpu.VMEM((tensor, 1, columns), jnp.float32),
                pltpu.VMEM((tensor, 1, columns), jnp.float32),
                pltpu.SemaphoreType.REGULAR((seq // (4 * ny),)),
                pltpu.SemaphoreType.REGULAR((2,)),
                dma((10,)),
                dma, dma, dma,
                dma((2,)),
                dma((2,)),
                dma((2,)),
                dma, dma,
                dma((tensor,)),
                dma((tensor,)),
            ],
            compiler_params=pltpu.CompilerParams(collective_id=0, has_side_effects=True),
        )(page_owner, page_fill, query, cache, w_uk, w_uv, w_out)

    return jax.shard_map(
        shards,
        mesh=mesh,
        in_specs=(
            P("seq", "tensor"), P("seq"), P("seq"), P("seq", None, None),
            P("tensor", None, None), P("tensor", None, None), P("tensor", None),
        ),
        out_specs=P("seq", "tensor"),
        check_vma=False,
    )
```

```python
import functools
import math

import jax
import jax.numpy as jnp
from jax import lax
from jax.experimental import pallas as pl
from jax.experimental.pallas import tpu as pltpu
from jax.sharding import PartitionSpec as P

MESH = pl.DeviceIdType.MESH
EMPTY = -1e30
LANES = 128
ROWS = 8
SENT = 6
NY = 8


def kernel(
    seq, tensor, scale, ny, nz,
    owner_hbm, fill_hbm, q_hbm, cache_hbm, wuk_hbm, wuv_hbm, wout_hbm,
    out_ref,
    owner, fill, q_ref, qmine, qearly, qlate, cache, wuk, wuv, wout, vproj, bias, sel, pick, sendb, recvb, rf, xs, xr,
    chip_in, line_in, local_sems, send1, recv1, send2, recv2, send3, recv3, bsend, brecv, xsend, xrecv,
):
    pages, page, width = cache.shape
    heads, nope, latent = wuk.shape
    rope = width - latent
    tokens = pages * page
    columns = wout.shape[2]
    me = lax.axis_index("seq")
    tx = lax.axis_index("tensor")
    core = lax.rem(me, 2)
    y = lax.rem(lax.div(me, 2), ny)
    z = lax.div(me, 2 * ny)
    deep = nz // 2
    late = lax.div(z, deep)
    line = z * 2 + core
    near = core * deep * ny
    block = near + lax.rem(z, deep) * ny
    half = seq // 2

    def along_y(k):
        return (z * ny + lax.rem(y + k, ny)) * 2 + core

    def in_half(part, k):
        at = part * 2 * deep + lax.rem(line + k, 2 * deep)
        return (lax.div(at, 2) * ny + y) * 2 + lax.rem(at, 2)

    small = [
        pltpu.make_async_copy(src, dst, local_sems.at[i])
        for i, (src, dst) in enumerate(((q_hbm, q_ref), (owner_hbm, owner), (fill_hbm, fill)))
    ]
    small[0].start()

    barrier = pltpu.get_barrier_semaphore()

    def tell(sem, peer):
        pl.semaphore_signal(sem, 1, device_id={"seq": peer}, device_id_type=MESH)

    def tell_half(sem, part, others_only):
        for k in range(2 * deep):
            peer = in_half(part, k)
            if others_only and k == 0:
                continue
            tell(sem, peer)

    def like_core(part, k):
        return ((part * deep + lax.rem(z + k, deep)) * ny + y) * 2 + core

    def tell_tensor(seat):
        for k in range(1, tensor):
            pl.semaphore_signal(
                barrier, 1,
                device_id={"seq": seat, "tensor": lax.rem(tx + k, tensor)},
                device_id_type=MESH,
            )

    first_core, sibling = me - core, me + 1 - 2 * core

    @pl.when(late == 0)
    def _():
        for k in range(1, ny):
            tell(barrier, along_y(k))
        tell_half(barrier, 0, True)
        for k in range(deep):
            tell(barrier, (deep + lax.rem(z + k, deep)) * 2 * ny + y * 2)
        tell_tensor(me)

    @pl.when(late == 1)
    def _():
        tell(barrier, sibling)
        for k in range(1, ny):
            tell(barrier, along_y(k) + 1 - core)
        tell_tensor(first_core + 1)

    small[1].start()
    small[2].start()

    @pl.when((late == 1) & (core == 0))
    def _():
        pl.semaphore_wait(barrier, 2 * deep + 1)
        for k in range(2 * deep):
            tell(chip_in.at[z - deep], in_half(0, k))
        tell(line_in.at[0], sibling)

    small[0].wait()
    q = q_ref[...].astype(jnp.float32)
    step = nope + rope
    rows = [q[:, h * step : h * step + nope] for h in range(heads)]
    ropes = [q[:, h * step + nope : (h + 1) * step] for h in range(heads)]
    rows += [jnp.concatenate(ropes[h : h + 2], axis=1) for h in range(0, heads, 2)]
    rows += [jnp.zeros((ROWS - SENT, LANES), jnp.float32)]
    qmine[...] = jnp.concatenate(rows, axis=0).astype(jnp.bfloat16)[None]
    loads = [
        pltpu.make_async_copy(src, dst, local_sems.at[3 + i])
        for i, (src, dst) in enumerate(
            ((wuk_hbm, wuk), (cache_hbm, cache), (wuv_hbm, wuv))
            + tuple((wout_hbm.at[:, pl.ds(t * columns, columns)], wout.at[t]) for t in range(tensor))
        )
    ]
    queries = (qearly, qlate)
    sent = pl.ds(0, SENT)

    @pl.when(late == 0)
    def _():
        pl.semaphore_wait(barrier, ny - 1 + 2 * deep - 1 + tensor - 1)

    @pl.when((late == 1) & (core == 1))
    def _():
        pl.semaphore_wait(barrier, 2 * (ny - 1) + 2 * (tensor - 1) + 1)
        tell(line_in.at[0], sibling)

    @pl.when(late == 1)
    def _():
        pl.semaphore_wait(line_in.at[0], 1)

    for part, buf in enumerate(queries):

        @pl.when(late == part)
        def _(buf=buf):
            mine = buf.at[pl.ds(block + y, 1), sent]
            for k in range(1, ny):
                pltpu.make_async_remote_copy(
                    src_ref=qmine.at[:, sent],
                    dst_ref=mine,
                    send_sem=send1,
                    recv_sem=recv1,
                    device_id={"seq": along_y(k)},
                    device_id_type=MESH,
                ).start()
            pltpu.make_async_copy(qmine.at[:, sent], mine, recv1).start()

    for load in loads:
        load.start()

    small[1].wait()
    small[2].wait()
    row16 = lax.broadcasted_iota(jnp.int32, (pages, LANES), 0)
    lane16 = lax.broadcasted_iota(jnp.int32, (pages, LANES), 1)
    own_row = jnp.zeros((pages, LANES), jnp.int32)
    own_lane = jnp.zeros((pages, LANES), jnp.int32)
    for p in range(pages):
        own_row = jnp.where(row16 == p, owner[p], own_row)
        own_lane = jnp.where((lane16 & (pages - 1)) == p, owner[p], own_lane)
    repeated = jnp.max(
        jnp.where((own_row == own_lane) & (row16 < (lane16 & (pages - 1))), 1, 0),
        axis=0, keepdims=True,
    )
    first_lane = jnp.where(repeated > 0, -1, own_lane[:1])
    big_row = lax.broadcasted_iota(jnp.int32, (seq * ROWS, LANES), 0)
    big_lane = lax.broadcasted_iota(jnp.int32, (seq * ROWS, LANES), 1)
    wanted = (first_lane * ROWS) + lax.div(big_lane[:1], pages)
    wanted = jnp.where((first_lane >= 0) & (big_lane[:1] < (heads + 1) * pages), wanted, -1)
    pick[...] = jnp.where(big_row == wanted, 1.0, 0.0).astype(jnp.bfloat16)
    own_rows = jnp.concatenate([own_row] * heads, axis=0)
    lane = lax.broadcasted_iota(jnp.int32, (1, LANES), 1)
    per = LANES // page
    for j in range(tokens // LANES):
        own_l = jnp.where(lane < page, owner[per * j], owner[per * j + 1])
        fill_l = jnp.where(lane < page, fill[per * j], fill[per * j + 1])
        own_l = jnp.where((lane & (page - 1)) < fill_l, own_l, -1)
        bias[:, j * LANES : (j + 1) * LANES] = jnp.where(own_rows == own_l, 0.0, EMPTY)

    def send_line(part, peers):
        mine = queries[part].at[pl.ds(block, ny), sent]
        for peer in peers:
            pltpu.make_async_remote_copy(
                src_ref=mine,
                dst_ref=mine,
                send_sem=send2,
                recv_sem=recv2.at[part],
                device_id={"seq": peer},
                device_id_type=MESH,
            ).start()

    for part, buf in enumerate(queries):

        @pl.when(late == part)
        def _(part=part, buf=buf):
            mine = buf.at[pl.ds(block, ny), sent]
            pltpu.make_async_copy(mine, mine, recv1).wait()
            if part == 0:
                send_line(0, [like_core(0, k) for k in range(1, deep)])
                for j in range(deep):
                    pl.semaphore_wait(chip_in.at[j], 1)
                    send_line(0, [((deep + j) * ny + y) * 2 + core])
                for k in range(2 * deep):
                    tell(line_in.at[1], in_half(1, k))
            else:
                send_line(1, [like_core(0, k) for k in range(deep)])
                pl.semaphore_wait(line_in.at[1], 2 * deep)
                send_line(1, [like_core(1, k) for k in range(1, deep)])

    loads[1].wait()
    loads[2].wait()
    keys = cache[...].reshape(tokens, width)
    for h in range(heads):
        vproj[:, h * LANES : (h + 1) * LANES] = jnp.dot(
            keys[:, :latent], wuv[h], preferred_element_type=jnp.float32
        ).astype(jnp.bfloat16)

    swaps = []
    for part, buf in enumerate(queries):
        for own, lines in ((part, deep - 1), (1 - part, deep)):

            @pl.when(late == own)
            def _(part=part, buf=buf, lines=lines):
                rest = buf.at[pl.ds(0, lines * ny), sent]
                pltpu.make_async_copy(rest, rest, recv2.at[part]).wait()

        heard = buf.at[pl.ds(near, deep * ny), sent]
        swap = pltpu.make_async_remote_copy(
            src_ref=heard,
            dst_ref=heard,
            send_sem=send3.at[part],
            recv_sem=recv3.at[part],
            device_id={"seq": sibling},
            device_id_type=MESH,
        )
        swap.start()
        swaps.append(swap)
        swap.wait_recv()

        for p in range(pages):
            spot = owner[p] & (half - 1)
            at = ((spot & 1) * deep + spot // (2 * ny)) * ny + ((spot // 2) & (ny - 1))
            sel[p * ROWS : (p + 1) * ROWS, :] = buf[at].astype(jnp.float32)
        if part == 0:
            loads[0].wait()
        joined = []
        for h in range(heads):
            plain = sel[pl.ds(h, pages, stride=ROWS), :].astype(jnp.bfloat16)
            pair = sel[pl.ds(heads + h // 2, pages, stride=ROWS), :]
            turned = pair[:, (h % 2) * rope : (h % 2 + 1) * rope].astype(jnp.bfloat16)
            lat = jnp.dot(plain, wuk[h], preferred_element_type=jnp.float32)
            joined.append(jnp.concatenate([lat.astype(jnp.bfloat16), turned], axis=1))
        joined = jnp.concatenate(joined, axis=0)

        keys = cache[...].reshape(tokens, width)
        scores = lax.dot_general(
            joined, keys, (((1,), (1,)), ((), ())), preferred_element_type=jnp.float32
        )
        scores = scores * scale + bias[...]
        top = jnp.max(scores, axis=1, keepdims=True)
        top = jnp.where(top > 0.5 * EMPTY, top, 0.0)
        top_hi = top.astype(jnp.bfloat16).astype(jnp.float32)
        top_lo = (top - top_hi).astype(jnp.bfloat16).astype(jnp.float32)
        weights = jnp.exp(scores - (top_hi + top_lo))
        total = jnp.sum(weights, axis=1, keepdims=True)
        total_hi = total.astype(jnp.bfloat16).astype(jnp.float32)
        total_lo = total - total_hi
        sums = jnp.dot(
            weights.astype(jnp.bfloat16), vproj[...], preferred_element_type=jnp.float32
        )

        blocks = [
            sums[h * pages : (h + 1) * pages, h * LANES : (h + 1) * LANES] for h in range(heads)
        ]
        stats = jnp.zeros((pages, LANES), jnp.float32)
        for i, piece in enumerate((top_hi, top_lo, total_hi, total_lo)):
            for h in range(heads):
                stats = jnp.where(
                    lane16 == i * heads + h, piece[h * pages : (h + 1) * pages], stats
                )
        blocks += [stats, jnp.zeros((LANES - (heads + 1) * pages, LANES), jnp.float32)]
        table = jnp.concatenate(blocks, axis=0).astype(jnp.bfloat16)
        def send_sums(k, c, base):
            peer = base + lax.rem(me + k, 2 * ny)
            pltpu.make_async_remote_copy(
                src_ref=sendb.at[peer, sent],
                dst_ref=recvb.at[me, sent],
                send_sem=bsend,
                recv_sem=brecv,
                device_id={"seq": peer},
                device_id_type=MESH,
            ).start()
            return c

        for level in range(part * deep, (part + 1) * deep):
            many = 2 * ny
            sendb[pl.ds(level * many, many)] = (
                jnp.dot(
                    pick[pl.ds(level * many * ROWS, many * ROWS), :], table,
                    preferred_element_type=jnp.float32,
                )
                .astype(jnp.bfloat16)
                .reshape(many, ROWS, LANES)
            )
            lax.fori_loop(
                jnp.where(z == level, 1, 0), 2 * ny,
                functools.partial(send_sums, base=level * 2 * ny), 0,
            )

    recvb[me] = sendb[me]
    others = recvb.at[pl.ds(0, seq - 1), sent]
    pltpu.make_async_copy(others, others, brecv).wait()

    rf[...] = recvb[...].reshape(seq * ROWS, LANES).astype(jnp.float32)
    got = rf[pl.ds(heads, seq, stride=ROWS), :]
    tops = got + pltpu.roll(got, LANES - heads, 1)
    totals = pltpu.roll(got, LANES - 2 * heads, 1) + pltpu.roll(got, LANES - 3 * heads, 1)
    some = totals > 0.0
    tops = jnp.where(some, tops, EMPTY)
    peak = jnp.max(tops, axis=0, keepdims=True)
    share = jnp.where(some, jnp.exp(tops - peak), 0.0)
    denominator = jnp.sum(jnp.where(some, share * totals, 0.0), axis=0, keepdims=True)
    outs = []
    for h in range(heads):
        mine = rf[pl.ds(h, seq, stride=ROWS), :]
        numerator = jnp.sum(mine * share[:, h : h + 1], axis=0, keepdims=True)
        outs.append(numerator / denominator[:, h : h + 1])
    head_out = jnp.concatenate(outs, axis=1).astype(jnp.bfloat16)

    for load in loads[3:]:
        load.wait()
    sends = []
    for k in [2, 1, 3, 0]:
        peer = lax.rem(tx + k, tensor)
        piece = jnp.dot(head_out, wout[peer], preferred_element_type=jnp.float32)
        if k == 0:
            xr[tx] = piece
            continue
        xs[peer] = piece
        sends.append(
            pltpu.make_async_remote_copy(
                src_ref=xs.at[peer],
                dst_ref=xr.at[tx],
                send_sem=xsend.at[k],
                recv_sem=xrecv.at[k],
                device_id={"tensor": peer},
                device_id_type=MESH,
            )
        )
        sends[-1].start()
    for send in sends:
        send.wait_recv()
    total_value = xr[0]
    for t in range(1, tensor):
        total_value = total_value + xr[t]
    out_ref[...] = total_value.astype(out_ref.dtype)
    for send in sends:
        send.wait_send()
    away = qearly.at[pl.ds(0, ny - 1), sent]
    pltpu.make_async_copy(away, away, send1).wait()
    away = qearly.at[pl.ds(0, (nz - 1) * ny), sent]
    pltpu.make_async_copy(away, away, send2).wait()
    for swap in swaps:
        swap.wait_send()
    away = sendb.at[pl.ds(0, seq - 1), sent]
    pltpu.make_async_copy(away, away, bsend).wait()


def solution(mesh):
    seq, tensor = mesh.shape["seq"], mesh.shape["tensor"]

    def shards(query, page_owner, page_fill, cache, w_uk, w_uv, w_out):
        heads = w_uk.shape[0]
        width = query.shape[1] // heads
        columns = w_out.shape[1] // tensor
        ny = NY

        def body(*refs):
            kernel(seq, tensor, 1.0 / math.sqrt(width), ny, seq // (2 * ny), *refs)

        vmem = pl.BlockSpec(memory_space=pltpu.VMEM)
        hbm = pl.BlockSpec(memory_space=pltpu.HBM)
        dma = pltpu.SemaphoreType.DMA
        return pl.pallas_call(
            body,
            out_shape=pltpu.VMEM((query.shape[0], columns), jnp.bfloat16),
            in_specs=[hbm] * 7,
            out_specs=vmem,
            scratch_shapes=[
                pltpu.SMEM(page_owner.shape, page_owner.dtype),
                pltpu.SMEM(page_fill.shape, page_fill.dtype),
                pltpu.VMEM(query.shape, query.dtype),
                pltpu.VMEM((1, ROWS, LANES), jnp.bfloat16),
                pltpu.VMEM((seq // 2, ROWS, LANES), jnp.bfloat16),
                pltpu.VMEM((seq // 2, ROWS, LANES), jnp.bfloat16),
                pltpu.VMEM(cache.shape, cache.dtype),
                pltpu.VMEM(w_uk.shape, w_uk.dtype),
                pltpu.VMEM(w_uv.shape, w_uv.dtype),
                pltpu.VMEM((tensor, w_out.shape[0], columns), w_out.dtype),
                pltpu.VMEM((cache.shape[0] * cache.shape[1], heads * LANES), jnp.bfloat16),
                pltpu.VMEM((page_owner.shape[0] * heads, cache.shape[0] * cache.shape[1]), jnp.float32),
                pltpu.VMEM((page_owner.shape[0] * ROWS, LANES), jnp.float32),
                pltpu.VMEM((seq * ROWS, LANES), jnp.bfloat16),
                pltpu.VMEM((seq, ROWS, LANES), jnp.bfloat16),
                pltpu.VMEM((seq, ROWS, LANES), jnp.bfloat16),
                pltpu.VMEM((seq * ROWS, LANES), jnp.float32),
                pltpu.VMEM((tensor, 1, columns), jnp.float32),
                pltpu.VMEM((tensor, 1, columns), jnp.float32),
                pltpu.SemaphoreType.REGULAR((seq // (4 * ny),)),
                pltpu.SemaphoreType.REGULAR((2,)),
                dma((10,)),
                dma, dma, dma,
                dma((2,)),
                dma((2,)),
                dma((2,)),
                dma, dma,
                dma((tensor,)),
                dma((tensor,)),
            ],
            compiler_params=pltpu.CompilerParams(collective_id=0, has_side_effects=True),
        )(page_owner, page_fill, query, cache, w_uk, w_uv, w_out)

    return jax.shard_map(
        shards,
        mesh=mesh,
        in_specs=(
            P("seq", "tensor"), P("seq"), P("seq"), P("seq", None, None),
            P("tensor", None, None), P("tensor", None, None), P("tensor", None),
        ),
        out_specs=P("seq", "tensor"),
        check_vma=False,
    )
```

```python
import functools
import math

import jax
import jax.numpy as jnp
from jax import lax
from jax.experimental import pallas as pl
from jax.experimental.pallas import tpu as pltpu
from jax.sharding import PartitionSpec as P

MESH = pl.DeviceIdType.MESH
EMPTY = -1e30
LANES = 128
ROWS = 8
SENT = 6
NY = 8


def kernel(
    seq, tensor, scale, ny, nz,
    owner_hbm, fill_hbm, q_hbm, cache_hbm, wuk_hbm, wuv_hbm, wout_hbm,
    out_ref,
    owner, fill, q_ref, qmine, qearly, qlate, cache, wuk, wuv, wout, vproj, bias, sel, pick, sendb, recvb, rf, xs, xr,
    chip_in, line_in, local_sems, send1, recv1, send2, recv2, send3, recv3, bsend, brecv, xsend, xrecv,
):
    pages, page, width = cache.shape
    heads, nope, latent = wuk.shape
    rope = width - latent
    tokens = pages * page
    columns = wout.shape[2]
    me = lax.axis_index("seq")
    tx = lax.axis_index("tensor")
    core = lax.rem(me, 2)
    y = lax.rem(lax.div(me, 2), ny)
    z = lax.div(me, 2 * ny)
    deep = nz // 2
    late = lax.div(z, deep)
    line = z * 2 + core
    near = core * deep * ny
    block = near + lax.rem(z, deep) * ny
    half = seq // 2

    def along_y(k):
        return (z * ny + lax.rem(y + k, ny)) * 2 + core

    def in_half(part, k):
        at = part * 2 * deep + lax.rem(line + k, 2 * deep)
        return (lax.div(at, 2) * ny + y) * 2 + lax.rem(at, 2)

    small = [
        pltpu.make_async_copy(src, dst, local_sems.at[i])
        for i, (src, dst) in enumerate(((q_hbm, q_ref), (owner_hbm, owner), (fill_hbm, fill)))
    ]
    small[0].start()

    barrier = pltpu.get_barrier_semaphore()

    def tell(sem, peer):
        pl.semaphore_signal(sem, 1, device_id={"seq": peer}, device_id_type=MESH)

    def tell_half(sem, part, others_only):
        for k in range(2 * deep):
            peer = in_half(part, k)
            if others_only and k == 0:
                continue
            tell(sem, peer)

    def like_core(part, k):
        return ((part * deep + lax.rem(z + k, deep)) * ny + y) * 2 + core

    def tell_tensor(seat):
        for k in range(1, tensor):
            pl.semaphore_signal(
                barrier, 1,
                device_id={"seq": seat, "tensor": lax.rem(tx + k, tensor)},
                device_id_type=MESH,
            )

    first_core, sibling = me - core, me + 1 - 2 * core

    @pl.when(late == 0)
    def _():
        for k in range(1, ny):
            tell(barrier, along_y(k))
        tell_half(barrier, 0, True)
        for k in range(deep):
            tell(barrier, (deep + lax.rem(z + k, deep)) * 2 * ny + y * 2)
        tell_tensor(me)

    @pl.when(late == 1)
    def _():
        tell(barrier, sibling)
        for k in range(1, ny):
            tell(barrier, along_y(k) + 1 - core)
        tell_tensor(first_core + 1)

    small[1].start()
    small[2].start()

    @pl.when((late == 1) & (core == 0))
    def _():
        pl.semaphore_wait(barrier, 2 * deep + 1)
        for k in range(2 * deep):
            tell(chip_in.at[z - deep], in_half(0, k))
        tell(line_in.at[0], sibling)

    small[0].wait()
    q = q_ref[...].astype(jnp.float32)
    step = nope + rope
    rows = [q[:, h * step : h * step + nope] for h in range(heads)]
    ropes = [q[:, h * step + nope : (h + 1) * step] for h in range(heads)]
    rows += [jnp.concatenate(ropes[h : h + 2], axis=1) for h in range(0, heads, 2)]
    rows += [jnp.zeros((ROWS - SENT, LANES), jnp.float32)]
    qmine[...] = jnp.concatenate(rows, axis=0).astype(jnp.bfloat16)[None]
    loads = [
        pltpu.make_async_copy(src, dst, local_sems.at[3 + i])
        for i, (src, dst) in enumerate(
            ((wuk_hbm, wuk), (cache_hbm, cache), (wuv_hbm, wuv))
            + tuple((wout_hbm.at[:, pl.ds(t * columns, columns)], wout.at[t]) for t in range(tensor))
        )
    ]
    queries = (qearly, qlate)
    sent = pl.ds(0, SENT)

    @pl.when(late == 0)
    def _():
        pl.semaphore_wait(barrier, ny - 1 + 2 * deep - 1 + tensor - 1)

    @pl.when((late == 1) & (core == 1))
    def _():
        pl.semaphore_wait(barrier, 2 * (ny - 1) + 2 * (tensor - 1) + 1)
        tell(line_in.at[0], sibling)

    @pl.when(late == 1)
    def _():
        pl.semaphore_wait(line_in.at[0], 1)

    for part, buf in enumerate(queries):

        @pl.when(late == part)
        def _(buf=buf):
            mine = buf.at[pl.ds(block + y, 1), sent]
            for k in range(1, ny):
                pltpu.make_async_remote_copy(
                    src_ref=qmine.at[:, sent],
                    dst_ref=mine,
                    send_sem=send1,
                    recv_sem=recv1,
                    device_id={"seq": along_y(k)},
                    device_id_type=MESH,
                ).start()
            pltpu.make_async_copy(qmine.at[:, sent], mine, recv1).start()

    for load in loads:
        load.start()

    small[1].wait()
    small[2].wait()
    row16 = lax.broadcasted_iota(jnp.int32, (pages, LANES), 0)
    lane16 = lax.broadcasted_iota(jnp.int32, (pages, LANES), 1)
    own_row = jnp.zeros((pages, LANES), jnp.int32)
    own_lane = jnp.zeros((pages, LANES), jnp.int32)
    for p in range(pages):
        own_row = jnp.where(row16 == p, owner[p], own_row)
        own_lane = jnp.where((lane16 & (pages - 1)) == p, owner[p], own_lane)
    repeated = jnp.max(
        jnp.where((own_row == own_lane) & (row16 < (lane16 & (pages - 1))), 1, 0),
        axis=0, keepdims=True,
    )
    first_lane = jnp.where(repeated > 0, -1, own_lane[:1])
    big_row = lax.broadcasted_iota(jnp.int32, (seq * ROWS, LANES), 0)
    big_lane = lax.broadcasted_iota(jnp.int32, (seq * ROWS, LANES), 1)
    wanted = (first_lane * ROWS) + lax.div(big_lane[:1], pages)
    wanted = jnp.where((first_lane >= 0) & (big_lane[:1] < (heads + 1) * pages), wanted, -1)
    pick[...] = jnp.where(big_row == wanted, 1.0, 0.0).astype(jnp.bfloat16)
    own_rows = jnp.concatenate([own_row] * heads, axis=0)
    lane = lax.broadcasted_iota(jnp.int32, (1, LANES), 1)
    per = LANES // page
    for j in range(tokens // LANES):
        own_l = jnp.where(lane < page, owner[per * j], owner[per * j + 1])
        fill_l = jnp.where(lane < page, fill[per * j], fill[per * j + 1])
        own_l = jnp.where((lane & (page - 1)) < fill_l, own_l, -1)
        bias[:, j * LANES : (j + 1) * LANES] = jnp.where(own_rows == own_l, 0.0, EMPTY)

    def send_line(part, peers):
        mine = queries[part].at[pl.ds(block, ny), sent]
        for peer in peers:
            pltpu.make_async_remote_copy(
                src_ref=mine,
                dst_ref=mine,
                send_sem=send2,
                recv_sem=recv2.at[part],
                device_id={"seq": peer},
                device_id_type=MESH,
            ).start()

    for part, buf in enumerate(queries):

        @pl.when(late == part)
        def _(part=part, buf=buf):
            mine = buf.at[pl.ds(block, ny), sent]
            pltpu.make_async_copy(mine, mine, recv1).wait()
            if part == 0:
                send_line(0, [like_core(0, k) for k in range(1, deep)])
                for j in range(deep):
                    pl.semaphore_wait(chip_in.at[j], 1)
                    send_line(0, [((deep + j) * ny + y) * 2 + core])
                for k in range(2 * deep):
                    tell(line_in.at[1], in_half(1, k))
            else:
                send_line(1, [like_core(0, k) for k in range(deep)])
                pl.semaphore_wait(line_in.at[1], 2 * deep)
                send_line(1, [like_core(1, k) for k in range(1, deep)])

    loads[1].wait()
    loads[2].wait()
    keys = cache[...].reshape(tokens, width)
    for h in range(heads):
        vproj[:, h * LANES : (h + 1) * LANES] = jnp.dot(
            keys[:, :latent], wuv[h], preferred_element_type=jnp.float32
        ).astype(jnp.bfloat16)

    swaps = []
    for part, buf in enumerate(queries):
        for own, lines in ((part, deep - 1), (1 - part, deep)):

            @pl.when(late == own)
            def _(part=part, buf=buf, lines=lines):
                rest = buf.at[pl.ds(0, lines * ny), sent]
                pltpu.make_async_copy(rest, rest, recv2.at[part]).wait()

        heard = buf.at[pl.ds(near, deep * ny), sent]
        swap = pltpu.make_async_remote_copy(
            src_ref=heard,
            dst_ref=heard,
            send_sem=send3.at[part],
            recv_sem=recv3.at[part],
            device_id={"seq": sibling},
            device_id_type=MESH,
        )
        swap.start()
        swaps.append(swap)
        swap.wait_recv()

        for p in range(pages):
            spot = owner[p] & (half - 1)
            at = ((spot & 1) * deep + spot // (2 * ny)) * ny + ((spot // 2) & (ny - 1))
            sel[p * ROWS : (p + 1) * ROWS, :] = buf[at].astype(jnp.float32)
        if part == 0:
            loads[0].wait()
        joined = []
        for h in range(heads):
            plain = sel[pl.ds(h, pages, stride=ROWS), :].astype(jnp.bfloat16)
            pair = sel[pl.ds(heads + h // 2, pages, stride=ROWS), :]
            turned = pair[:, (h % 2) * rope : (h % 2 + 1) * rope].astype(jnp.bfloat16)
            lat = jnp.dot(plain, wuk[h], preferred_element_type=jnp.float32)
            joined.append(jnp.concatenate([lat.astype(jnp.bfloat16), turned], axis=1))
        joined = jnp.concatenate(joined, axis=0)

        keys = cache[...].reshape(tokens, width)
        scores = lax.dot_general(
            joined, keys, (((1,), (1,)), ((), ())), preferred_element_type=jnp.float32
        )
        scores = scores * scale + bias[...]
        top = jnp.max(scores, axis=1, keepdims=True)
        top = jnp.where(top > 0.5 * EMPTY, top, 0.0)
        top_hi = top.astype(jnp.bfloat16).astype(jnp.float32)
        top_lo = (top - top_hi).astype(jnp.bfloat16).astype(jnp.float32)
        weights = jnp.exp(scores - (top_hi + top_lo))
        total = jnp.sum(weights, axis=1, keepdims=True)
        total_hi = total.astype(jnp.bfloat16).astype(jnp.float32)
        total_lo = total - total_hi
        sums = jnp.dot(
            weights.astype(jnp.bfloat16), vproj[...], preferred_element_type=jnp.float32
        )

        blocks = [
            sums[h * pages : (h + 1) * pages, h * LANES : (h + 1) * LANES] for h in range(heads)
        ]
        stats = jnp.zeros((pages, LANES), jnp.float32)
        for i, piece in enumerate((top_hi, top_lo, total_hi, total_lo)):
            for h in range(heads):
                stats = jnp.where(
                    lane16 == i * heads + h, piece[h * pages : (h + 1) * pages], stats
                )
        blocks += [stats, jnp.zeros((LANES - (heads + 1) * pages, LANES), jnp.float32)]
        table = jnp.concatenate(blocks, axis=0).astype(jnp.bfloat16)
        def send_sums(k, c, base):
            peer = base + k

            @pl.when(peer != me)
            def _():
                pltpu.make_async_remote_copy(
                    src_ref=sendb.at[peer, sent],
                    dst_ref=recvb.at[me, sent],
                    send_sem=bsend,
                    recv_sem=brecv,
                    device_id={"seq": peer},
                    device_id_type=MESH,
                ).start()

            return c

        for level in range(part * deep, (part + 1) * deep):
            many = 2 * ny
            sendb[pl.ds(level * many, many)] = (
                jnp.dot(
                    pick[pl.ds(level * many * ROWS, many * ROWS), :], table,
                    preferred_element_type=jnp.float32,
                )
                .astype(jnp.bfloat16)
                .reshape(many, ROWS, LANES)
            )
            lax.fori_loop(
                0, 2 * ny,
                functools.partial(send_sums, base=level * 2 * ny), 0,
            )

    recvb[me] = sendb[me]
    others = recvb.at[pl.ds(0, seq - 1), sent]
    pltpu.make_async_copy(others, others, brecv).wait()

    rf[...] = recvb[...].reshape(seq * ROWS, LANES).astype(jnp.float32)
    got = rf[pl.ds(heads, seq, stride=ROWS), :]
    tops = got + pltpu.roll(got, LANES - heads, 1)
    totals = pltpu.roll(got, LANES - 2 * heads, 1) + pltpu.roll(got, LANES - 3 * heads, 1)
    some = totals > 0.0
    tops = jnp.where(some, tops, EMPTY)
    peak = jnp.max(tops, axis=0, keepdims=True)
    share = jnp.where(some, jnp.exp(tops - peak), 0.0)
    denominator = jnp.sum(jnp.where(some, share * totals, 0.0), axis=0, keepdims=True)
    outs = []
    for h in range(heads):
        mine = rf[pl.ds(h, seq, stride=ROWS), :]
        numerator = jnp.sum(mine * share[:, h : h + 1], axis=0, keepdims=True)
        outs.append(numerator / denominator[:, h : h + 1])
    head_out = jnp.concatenate(outs, axis=1).astype(jnp.bfloat16)

    for load in loads[3:]:
        load.wait()
    sends = []
    for k in [2, 1, 3, 0]:
        peer = lax.rem(tx + k, tensor)
        piece = jnp.dot(head_out, wout[peer], preferred_element_type=jnp.float32)
        if k == 0:
            xr[tx] = piece
            continue
        xs[peer] = piece
        sends.append(
            pltpu.make_async_remote_copy(
                src_ref=xs.at[peer],
                dst_ref=xr.at[tx],
                send_sem=xsend.at[k],
                recv_sem=xrecv.at[k],
                device_id={"tensor": peer},
                device_id_type=MESH,
            )
        )
        sends[-1].start()
    for send in sends:
        send.wait_recv()
    total_value = xr[0]
    for t in range(1, tensor):
        total_value = total_value + xr[t]
    out_ref[...] = total_value.astype(out_ref.dtype)
    for send in sends:
        send.wait_send()
    away = qearly.at[pl.ds(0, ny - 1), sent]
    pltpu.make_async_copy(away, away, send1).wait()
    away = qearly.at[pl.ds(0, (nz - 1) * ny), sent]
    pltpu.make_async_copy(away, away, send2).wait()
    for swap in swaps:
        swap.wait_send()
    away = sendb.at[pl.ds(0, seq - 1), sent]
    pltpu.make_async_copy(away, away, bsend).wait()


def solution(mesh):
    seq, tensor = mesh.shape["seq"], mesh.shape["tensor"]

    def shards(query, page_owner, page_fill, cache, w_uk, w_uv, w_out):
        heads = w_uk.shape[0]
        width = query.shape[1] // heads
        columns = w_out.shape[1] // tensor
        ny = NY

        def body(*refs):
            kernel(seq, tensor, 1.0 / math.sqrt(width), ny, seq // (2 * ny), *refs)

        vmem = pl.BlockSpec(memory_space=pltpu.VMEM)
        hbm = pl.BlockSpec(memory_space=pltpu.HBM)
        dma = pltpu.SemaphoreType.DMA
        return pl.pallas_call(
            body,
            out_shape=pltpu.VMEM((query.shape[0], columns), jnp.bfloat16),
            in_specs=[hbm] * 7,
            out_specs=vmem,
            scratch_shapes=[
                pltpu.SMEM(page_owner.shape, page_owner.dtype),
                pltpu.SMEM(page_fill.shape, page_fill.dtype),
                pltpu.VMEM(query.shape, query.dtype),
                pltpu.VMEM((1, ROWS, LANES), jnp.bfloat16),
                pltpu.VMEM((seq // 2, ROWS, LANES), jnp.bfloat16),
                pltpu.VMEM((seq // 2, ROWS, LANES), jnp.bfloat16),
                pltpu.VMEM(cache.shape, cache.dtype),
                pltpu.VMEM(w_uk.shape, w_uk.dtype),
                pltpu.VMEM(w_uv.shape, w_uv.dtype),
                pltpu.VMEM((tensor, w_out.shape[0], columns), w_out.dtype),
                pltpu.VMEM((cache.shape[0] * cache.shape[1], heads * LANES), jnp.bfloat16),
                pltpu.VMEM((page_owner.shape[0] * heads, cache.shape[0] * cache.shape[1]), jnp.float32),
                pltpu.VMEM((page_owner.shape[0] * ROWS, LANES), jnp.float32),
                pltpu.VMEM((seq * ROWS, LANES), jnp.bfloat16),
                pltpu.VMEM((seq, ROWS, LANES), jnp.bfloat16),
                pltpu.VMEM((seq, ROWS, LANES), jnp.bfloat16),
                pltpu.VMEM((seq * ROWS, LANES), jnp.float32),
                pltpu.VMEM((tensor, 1, columns), jnp.float32),
                pltpu.VMEM((tensor, 1, columns), jnp.float32),
                pltpu.SemaphoreType.REGULAR((seq // (4 * ny),)),
                pltpu.SemaphoreType.REGULAR((2,)),
                dma((10,)),
                dma, dma, dma,
                dma((2,)),
                dma((2,)),
                dma((2,)),
                dma, dma,
                dma((tensor,)),
                dma((tensor,)),
            ],
            compiler_params=pltpu.CompilerParams(collective_id=0, has_side_effects=True),
        )(page_owner, page_fill, query, cache, w_uk, w_uv, w_out)

    return jax.shard_map(
        shards,
        mesh=mesh,
        in_specs=(
            P("seq", "tensor"), P("seq"), P("seq"), P("seq", None, None),
            P("tensor", None, None), P("tensor", None, None), P("tensor", None),
        ),
        out_specs=P("seq", "tensor"),
        check_vma=False,
    )
```

```python
import functools
import math

import jax
import jax.numpy as jnp
from jax import lax
from jax.experimental import pallas as pl
from jax.experimental.pallas import tpu as pltpu
from jax.sharding import PartitionSpec as P

MESH = pl.DeviceIdType.MESH
EMPTY = -1e30
LANES = 128
ROWS = 8
SENT = 6
NY = 8


def kernel(
    seq, tensor, scale, ny, nz,
    owner_hbm, fill_hbm, q_hbm, cache_hbm, wuk_hbm, wuv_hbm, wout_hbm,
    out_ref,
    owner, fill, q_ref, qmine, qearly, qlate, cache, wuk, wuv, wout, vproj, bias, sel, pick, sendb, recvb, rf, xs, xr,
    chip_in, line_in, local_sems, send1, recv1, send2, recv2, send3, recv3, bsend, brecv, xsend, xrecv,
):
    pages, page, width = cache.shape
    heads, nope, latent = wuk.shape
    rope = width - latent
    tokens = pages * page
    columns = wout.shape[2]
    me = lax.axis_index("seq")
    tx = lax.axis_index("tensor")
    core = lax.rem(me, 2)
    y = lax.rem(lax.div(me, 2), ny)
    z = lax.div(me, 2 * ny)
    deep = nz // 2
    late = lax.div(z, deep)
    line = z * 2 + core
    near = core * deep * ny
    block = near + lax.rem(z, deep) * ny
    half = seq // 2

    far_first = sorted(range(1, ny), key=lambda k: -min(k, ny - k))

    def along_y(k):
        return (z * ny + lax.rem(y + k, ny)) * 2 + core

    def in_half(part, k):
        at = part * 2 * deep + lax.rem(line + k, 2 * deep)
        return (lax.div(at, 2) * ny + y) * 2 + lax.rem(at, 2)

    small = [
        pltpu.make_async_copy(src, dst, local_sems.at[i])
        for i, (src, dst) in enumerate(((q_hbm, q_ref), (owner_hbm, owner), (fill_hbm, fill)))
    ]
    small[0].start()

    barrier = pltpu.get_barrier_semaphore()

    def tell(sem, peer):
        pl.semaphore_signal(sem, 1, device_id={"seq": peer}, device_id_type=MESH)

    def tell_half(sem, part, others_only):
        for k in range(2 * deep):
            peer = in_half(part, k)
            if others_only and k == 0:
                continue
            tell(sem, peer)

    def like_core(part, k):
        return ((part * deep + lax.rem(z + k, deep)) * ny + y) * 2 + core

    def tell_tensor(seat):
        for k in range(1, tensor):
            pl.semaphore_signal(
                barrier, 1,
                device_id={"seq": seat, "tensor": lax.rem(tx + k, tensor)},
                device_id_type=MESH,
            )

    first_core, sibling = me - core, me + 1 - 2 * core

    @pl.when(late == 0)
    def _():
        for k in far_first:
            tell(barrier, along_y(k))
        tell_tensor(me)
        tell_half(barrier, 0, True)
        for k in range(deep):
            tell(barrier, (deep + lax.rem(z + k, deep)) * 2 * ny + y * 2)

    @pl.when(late == 1)
    def _():
        tell(barrier, sibling)
        for k in far_first:
            tell(barrier, along_y(k) + 1 - core)
        tell_tensor(first_core + 1)

    small[1].start()
    small[2].start()

    @pl.when((late == 1) & (core == 0))
    def _():
        pl.semaphore_wait(barrier, 2 * deep + 1)
        for k in range(2 * deep):
            tell(chip_in.at[z - deep], in_half(0, k))
        tell(line_in.at[0], sibling)

    small[0].wait()
    q = q_ref[...].astype(jnp.float32)
    step = nope + rope
    rows = [q[:, h * step : h * step + nope] for h in range(heads)]
    ropes = [q[:, h * step + nope : (h + 1) * step] for h in range(heads)]
    rows += [jnp.concatenate(ropes[h : h + 2], axis=1) for h in range(0, heads, 2)]
    rows += [jnp.zeros((ROWS - SENT, LANES), jnp.float32)]
    qmine[...] = jnp.concatenate(rows, axis=0).astype(jnp.bfloat16)[None]
    loads = [
        pltpu.make_async_copy(src, dst, local_sems.at[3 + i])
        for i, (src, dst) in enumerate(
            ((wuk_hbm, wuk), (cache_hbm, cache), (wuv_hbm, wuv))
            + tuple((wout_hbm.at[:, pl.ds(t * columns, columns)], wout.at[t]) for t in range(tensor))
        )
    ]
    queries = (qearly, qlate)
    sent = pl.ds(0, SENT)

    @pl.when(late == 0)
    def _():
        pl.semaphore_wait(barrier, ny - 1 + 2 * deep - 1 + tensor - 1)

    @pl.when((late == 1) & (core == 1))
    def _():
        pl.semaphore_wait(barrier, 2 * (ny - 1) + 2 * (tensor - 1) + 1)
        tell(line_in.at[0], sibling)

    @pl.when(late == 1)
    def _():
        pl.semaphore_wait(line_in.at[0], 1)

    for part, buf in enumerate(queries):

        @pl.when(late == part)
        def _(buf=buf):
            mine = buf.at[pl.ds(block + y, 1), sent]
            for k in far_first:
                pltpu.make_async_remote_copy(
                    src_ref=qmine.at[:, sent],
                    dst_ref=mine,
                    send_sem=send1,
                    recv_sem=recv1,
                    device_id={"seq": along_y(k)},
                    device_id_type=MESH,
                ).start()
            pltpu.make_async_copy(qmine.at[:, sent], mine, recv1).start()

    for load in loads:
        load.start()

    small[1].wait()
    small[2].wait()
    row16 = lax.broadcasted_iota(jnp.int32, (pages, LANES), 0)
    lane16 = lax.broadcasted_iota(jnp.int32, (pages, LANES), 1)
    own_row = jnp.zeros((pages, LANES), jnp.int32)
    own_lane = jnp.zeros((pages, LANES), jnp.int32)
    for p in range(pages):
        own_row = jnp.where(row16 == p, owner[p], own_row)
        own_lane = jnp.where((lane16 & (pages - 1)) == p, owner[p], own_lane)
    repeated = jnp.max(
        jnp.where((own_row == own_lane) & (row16 < (lane16 & (pages - 1))), 1, 0),
        axis=0, keepdims=True,
    )
    first_lane = jnp.where(repeated > 0, -1, own_lane[:1])
    big_row = lax.broadcasted_iota(jnp.int32, (seq * ROWS, LANES), 0)
    big_lane = lax.broadcasted_iota(jnp.int32, (seq * ROWS, LANES), 1)
    wanted = (first_lane * ROWS) + lax.div(big_lane[:1], pages)
    wanted = jnp.where((first_lane >= 0) & (big_lane[:1] < (heads + 1) * pages), wanted, -1)
    pick[...] = jnp.where(big_row == wanted, 1.0, 0.0).astype(jnp.bfloat16)
    own_rows = jnp.concatenate([own_row] * heads, axis=0)
    lane = lax.broadcasted_iota(jnp.int32, (1, LANES), 1)
    per = LANES // page
    for j in range(tokens // LANES):
        own_l = jnp.where(lane < page, owner[per * j], owner[per * j + 1])
        fill_l = jnp.where(lane < page, fill[per * j], fill[per * j + 1])
        own_l = jnp.where((lane & (page - 1)) < fill_l, own_l, -1)
        bias[:, j * LANES : (j + 1) * LANES] = jnp.where(own_rows == own_l, 0.0, EMPTY)

    def send_line(part, peers):
        mine = queries[part].at[pl.ds(block, ny), sent]
        for peer in peers:
            pltpu.make_async_remote_copy(
                src_ref=mine,
                dst_ref=mine,
                send_sem=send2,
                recv_sem=recv2.at[part],
                device_id={"seq": peer},
                device_id_type=MESH,
            ).start()

    for part, buf in enumerate(queries):

        @pl.when(late == part)
        def _(part=part, buf=buf):
            mine = buf.at[pl.ds(block, ny), sent]
            pltpu.make_async_copy(mine, mine, recv1).wait()
            if part == 0:
                send_line(0, [like_core(0, k) for k in range(1, deep)])
                for j in range(deep):
                    pl.semaphore_wait(chip_in.at[j], 1)
                    send_line(0, [((deep + j) * ny + y) * 2 + core])
                for k in range(2 * deep):
                    tell(line_in.at[1], in_half(1, k))
            else:
                send_line(1, [like_core(0, k) for k in range(deep)])
                pl.semaphore_wait(line_in.at[1], 2 * deep)
                send_line(1, [like_core(1, k) for k in range(1, deep)])

    loads[1].wait()
    loads[2].wait()
    keys = cache[...].reshape(tokens, width)
    for h in range(heads):
        vproj[:, h * LANES : (h + 1) * LANES] = jnp.dot(
            keys[:, :latent], wuv[h], preferred_element_type=jnp.float32
        ).astype(jnp.bfloat16)

    swaps = []
    for part, buf in enumerate(queries):
        for own, lines in ((part, deep - 1), (1 - part, deep)):

            @pl.when(late == own)
            def _(part=part, buf=buf, lines=lines):
                rest = buf.at[pl.ds(0, lines * ny), sent]
                pltpu.make_async_copy(rest, rest, recv2.at[part]).wait()

        heard = buf.at[pl.ds(near, deep * ny), sent]
        swap = pltpu.make_async_remote_copy(
            src_ref=heard,
            dst_ref=heard,
            send_sem=send3.at[part],
            recv_sem=recv3.at[part],
            device_id={"seq": sibling},
            device_id_type=MESH,
        )
        swap.start()
        swaps.append(swap)
        swap.wait_recv()

        for p in range(pages):
            spot = owner[p] & (half - 1)
            at = ((spot & 1) * deep + spot // (2 * ny)) * ny + ((spot // 2) & (ny - 1))
            sel[p * ROWS : (p + 1) * ROWS, :] = buf[at].astype(jnp.float32)
        if part == 0:
            loads[0].wait()
        joined = []
        for h in range(heads):
            plain = sel[pl.ds(h, pages, stride=ROWS), :].astype(jnp.bfloat16)
            pair = sel[pl.ds(heads + h // 2, pages, stride=ROWS), :]
            turned = pair[:, (h % 2) * rope : (h % 2 + 1) * rope].astype(jnp.bfloat16)
            lat = jnp.dot(plain, wuk[h], preferred_element_type=jnp.float32)
            joined.append(jnp.concatenate([lat.astype(jnp.bfloat16), turned], axis=1))
        joined = jnp.concatenate(joined, axis=0)

        keys = cache[...].reshape(tokens, width)
        scores = lax.dot_general(
            joined, keys, (((1,), (1,)), ((), ())), preferred_element_type=jnp.float32
        )
        scores = scores * scale + bias[...]
        top = jnp.max(scores, axis=1, keepdims=True)
        top = jnp.where(top > 0.5 * EMPTY, top, 0.0)
        top_hi = top.astype(jnp.bfloat16).astype(jnp.float32)
        top_lo = (top - top_hi).astype(jnp.bfloat16).astype(jnp.float32)
        weights = jnp.exp(scores - (top_hi + top_lo))
        total = jnp.sum(weights, axis=1, keepdims=True)
        total_hi = total.astype(jnp.bfloat16).astype(jnp.float32)
        total_lo = total - total_hi
        sums = jnp.dot(
            weights.astype(jnp.bfloat16), vproj[...], preferred_element_type=jnp.float32
        )

        blocks = [
            sums[h * pages : (h + 1) * pages, h * LANES : (h + 1) * LANES] for h in range(heads)
        ]
        stats = jnp.zeros((pages, LANES), jnp.float32)
        for i, piece in enumerate((top_hi, top_lo, total_hi, total_lo)):
            for h in range(heads):
                stats = jnp.where(
                    lane16 == i * heads + h, piece[h * pages : (h + 1) * pages], stats
                )
        blocks += [stats, jnp.zeros((LANES - (heads + 1) * pages, LANES), jnp.float32)]
        table = jnp.concatenate(blocks, axis=0).astype(jnp.bfloat16)
        def send_sums(k, c, base):
            peer = base + k

            @pl.when(peer != me)
            def _():
                pltpu.make_async_remote_copy(
                    src_ref=sendb.at[peer, sent],
                    dst_ref=recvb.at[me, sent],
                    send_sem=bsend,
                    recv_sem=brecv,
                    device_id={"seq": peer},
                    device_id_type=MESH,
                ).start()

            return c

        for level in range(part * deep, (part + 1) * deep):
            many = 2 * ny
            sendb[pl.ds(level * many, many)] = (
                jnp.dot(
                    pick[pl.ds(level * many * ROWS, many * ROWS), :], table,
                    preferred_element_type=jnp.float32,
                )
                .astype(jnp.bfloat16)
                .reshape(many, ROWS, LANES)
            )
            lax.fori_loop(
                0, 2 * ny,
                functools.partial(send_sums, base=level * 2 * ny), 0,
            )

    recvb[me] = sendb[me]
    others = recvb.at[pl.ds(0, seq - 1), sent]
    pltpu.make_async_copy(others, others, brecv).wait()

    rf[...] = recvb[...].reshape(seq * ROWS, LANES).astype(jnp.float32)
    got = rf[pl.ds(heads, seq, stride=ROWS), :]
    tops = got + pltpu.roll(got, LANES - heads, 1)
    totals = pltpu.roll(got, LANES - 2 * heads, 1) + pltpu.roll(got, LANES - 3 * heads, 1)
    some = totals > 0.0
    tops = jnp.where(some, tops, EMPTY)
    peak = jnp.max(tops, axis=0, keepdims=True)
    share = jnp.where(some, jnp.exp(tops - peak), 0.0)
    denominator = jnp.sum(jnp.where(some, share * totals, 0.0), axis=0, keepdims=True)
    outs = []
    for h in range(heads):
        mine = rf[pl.ds(h, seq, stride=ROWS), :]
        numerator = jnp.sum(mine * share[:, h : h + 1], axis=0, keepdims=True)
        outs.append(numerator / denominator[:, h : h + 1])
    head_out = jnp.concatenate(outs, axis=1).astype(jnp.bfloat16)

    for load in loads[3:]:
        load.wait()
    sends = []
    for k in [2, 1, 3, 0]:
        peer = lax.rem(tx + k, tensor)
        piece = jnp.dot(head_out, wout[peer], preferred_element_type=jnp.float32)
        if k == 0:
            xr[tx] = piece
            continue
        xs[peer] = piece
        sends.append(
            pltpu.make_async_remote_copy(
                src_ref=xs.at[peer],
                dst_ref=xr.at[tx],
                send_sem=xsend.at[k],
                recv_sem=xrecv.at[k],
                device_id={"tensor": peer},
                device_id_type=MESH,
            )
        )
        sends[-1].start()
    for send in sends:
        send.wait_recv()
    total_value = xr[0]
    for t in range(1, tensor):
        total_value = total_value + xr[t]
    out_ref[...] = total_value.astype(out_ref.dtype)
    for send in sends:
        send.wait_send()
    away = qearly.at[pl.ds(0, ny - 1), sent]
    pltpu.make_async_copy(away, away, send1).wait()
    away = qearly.at[pl.ds(0, (nz - 1) * ny), sent]
    pltpu.make_async_copy(away, away, send2).wait()
    for swap in swaps:
        swap.wait_send()
    away = sendb.at[pl.ds(0, seq - 1), sent]
    pltpu.make_async_copy(away, away, bsend).wait()


def solution(mesh):
    seq, tensor = mesh.shape["seq"], mesh.shape["tensor"]

    def shards(query, page_owner, page_fill, cache, w_uk, w_uv, w_out):
        heads = w_uk.shape[0]
        width = query.shape[1] // heads
        columns = w_out.shape[1] // tensor
        ny = NY

        def body(*refs):
            kernel(seq, tensor, 1.0 / math.sqrt(width), ny, seq // (2 * ny), *refs)

        vmem = pl.BlockSpec(memory_space=pltpu.VMEM)
        hbm = pl.BlockSpec(memory_space=pltpu.HBM)
        dma = pltpu.SemaphoreType.DMA
        return pl.pallas_call(
            body,
            out_shape=pltpu.VMEM((query.shape[0], columns), jnp.bfloat16),
            in_specs=[hbm] * 7,
            out_specs=vmem,
            scratch_shapes=[
                pltpu.SMEM(page_owner.shape, page_owner.dtype),
                pltpu.SMEM(page_fill.shape, page_fill.dtype),
                pltpu.VMEM(query.shape, query.dtype),
                pltpu.VMEM((1, ROWS, LANES), jnp.bfloat16),
                pltpu.VMEM((seq // 2, ROWS, LANES), jnp.bfloat16),
                pltpu.VMEM((seq // 2, ROWS, LANES), jnp.bfloat16),
                pltpu.VMEM(cache.shape, cache.dtype),
                pltpu.VMEM(w_uk.shape, w_uk.dtype),
                pltpu.VMEM(w_uv.shape, w_uv.dtype),
                pltpu.VMEM((tensor, w_out.shape[0], columns), w_out.dtype),
                pltpu.VMEM((cache.shape[0] * cache.shape[1], heads * LANES), jnp.bfloat16),
                pltpu.VMEM((page_owner.shape[0] * heads, cache.shape[0] * cache.shape[1]), jnp.float32),
                pltpu.VMEM((page_owner.shape[0] * ROWS, LANES), jnp.float32),
                pltpu.VMEM((seq * ROWS, LANES), jnp.bfloat16),
                pltpu.VMEM((seq, ROWS, LANES), jnp.bfloat16),
                pltpu.VMEM((seq, ROWS, LANES), jnp.bfloat16),
                pltpu.VMEM((seq * ROWS, LANES), jnp.float32),
                pltpu.VMEM((tensor, 1, columns), jnp.float32),
                pltpu.VMEM((tensor, 1, columns), jnp.float32),
                pltpu.SemaphoreType.REGULAR((seq // (4 * ny),)),
                pltpu.SemaphoreType.REGULAR((2,)),
                dma((10,)),
                dma, dma, dma,
                dma((2,)),
                dma((2,)),
                dma((2,)),
                dma, dma,
                dma((tensor,)),
                dma((tensor,)),
            ],
            compiler_params=pltpu.CompilerParams(collective_id=0, has_side_effects=True),
        )(page_owner, page_fill, query, cache, w_uk, w_uv, w_out)

    return jax.shard_map(
        shards,
        mesh=mesh,
        in_specs=(
            P("seq", "tensor"), P("seq"), P("seq"), P("seq", None, None),
            P("tensor", None, None), P("tensor", None, None), P("tensor", None),
        ),
        out_specs=P("seq", "tensor"),
        check_vma=False,
    )
```

```python
import functools
import math

import jax
import jax.numpy as jnp
from jax import lax
from jax.experimental import pallas as pl
from jax.experimental.pallas import tpu as pltpu
from jax.sharding import PartitionSpec as P

MESH = pl.DeviceIdType.MESH
EMPTY = -1e30
LANES = 128
ROWS = 8
SENT = 6
NY = 8


def kernel(
    seq, tensor, scale, ny, nz,
    owner_hbm, fill_hbm, q_hbm, cache_hbm, wuk_hbm, wuv_hbm, wout_hbm,
    out_ref,
    owner, fill, q_ref, qmine, qearly, qlate, cache, wuk, wuv, wout, vproj, bias, sel, pick, sendb, recvb, rf, xs, xr,
    chip_in, line_in, local_sems, send1, recv1, send2, recv2, send3, recv3, bsend, brecv, xsend, xrecv,
):
    pages, page, width = cache.shape
    heads, nope, latent = wuk.shape
    rope = width - latent
    tokens = pages * page
    columns = wout.shape[2]
    me = lax.axis_index("seq")
    tx = lax.axis_index("tensor")
    core = lax.rem(me, 2)
    y = lax.rem(lax.div(me, 2), ny)
    z = lax.div(me, 2 * ny)
    deep = nz // 2
    late = lax.div(z, deep)
    line = z * 2 + core
    near = core * deep * ny
    block = near + lax.rem(z, deep) * ny
    half = seq // 2

    far_first = sorted(range(1, ny), key=lambda k: -min(k, ny - k))

    def along_y(k):
        return (z * ny + lax.rem(y + k, ny)) * 2 + core

    def in_half(part, k):
        at = part * 2 * deep + lax.rem(line + k, 2 * deep)
        return (lax.div(at, 2) * ny + y) * 2 + lax.rem(at, 2)

    small = [
        pltpu.make_async_copy(src, dst, local_sems.at[i])
        for i, (src, dst) in enumerate(((q_hbm, q_ref), (owner_hbm, owner), (fill_hbm, fill)))
    ]
    small[0].start()

    barrier = pltpu.get_barrier_semaphore()

    def tell(sem, peer):
        pl.semaphore_signal(sem, 1, device_id={"seq": peer}, device_id_type=MESH)

    def tell_half(sem, part, others_only):
        for k in range(2 * deep):
            peer = in_half(part, k)
            if others_only and k == 0:
                continue
            tell(sem, peer)

    def like_core(part, k):
        return ((part * deep + lax.rem(z + k, deep)) * ny + y) * 2 + core

    def tell_tensor(seat):
        for k in range(1, tensor):
            pl.semaphore_signal(
                barrier, 1,
                device_id={"seq": seat, "tensor": lax.rem(tx + k, tensor)},
                device_id_type=MESH,
            )

    first_core, sibling = me - core, me + 1 - 2 * core

    @pl.when(late == 0)
    def _():
        for k in far_first:
            tell(barrier, along_y(k))
        tell_tensor(me)
        tell_half(barrier, 0, True)
        for k in range(deep):
            tell(barrier, (deep + lax.rem(z + k, deep)) * 2 * ny + y * 2)

    @pl.when(late == 1)
    def _():
        tell(barrier, sibling)
        for k in far_first:
            tell(barrier, along_y(k) + 1 - core)
        tell_tensor(first_core + 1)

    small[1].start()
    small[2].start()

    @pl.when((late == 1) & (core == 0))
    def _():
        pl.semaphore_wait(barrier, 2 * deep + 1)
        for k in range(2 * deep):
            tell(chip_in.at[z - deep], in_half(0, k))
        tell(line_in.at[0], sibling)

    small[0].wait()
    q = q_ref[...].astype(jnp.float32)
    step = nope + rope
    rows = [q[:, h * step : h * step + nope] for h in range(heads)]
    ropes = [q[:, h * step + nope : (h + 1) * step] for h in range(heads)]
    rows += [jnp.concatenate(ropes[h : h + 2], axis=1) for h in range(0, heads, 2)]
    rows += [jnp.zeros((ROWS - SENT, LANES), jnp.float32)]
    qmine[...] = jnp.concatenate(rows, axis=0).astype(jnp.bfloat16)[None]
    loads = [
        pltpu.make_async_copy(src, dst, local_sems.at[3 + i])
        for i, (src, dst) in enumerate(
            ((wuk_hbm, wuk), (cache_hbm, cache), (wuv_hbm, wuv))
            + tuple((wout_hbm.at[:, pl.ds(t * columns, columns)], wout.at[t]) for t in range(tensor))
        )
    ]
    queries = (qearly, qlate)
    sent = pl.ds(0, SENT)

    @pl.when(late == 0)
    def _():
        pl.semaphore_wait(barrier, ny - 1 + 2 * deep - 1 + tensor - 1)

    @pl.when((late == 1) & (core == 1))
    def _():
        pl.semaphore_wait(barrier, 2 * (ny - 1) + 2 * (tensor - 1) + 1)
        tell(line_in.at[0], sibling)

    @pl.when(late == 1)
    def _():
        pl.semaphore_wait(line_in.at[0], 1)

    for part, buf in enumerate(queries):

        @pl.when(late == part)
        def _(buf=buf):
            mine = buf.at[pl.ds(block + y, 1), sent]
            for k in far_first:
                pltpu.make_async_remote_copy(
                    src_ref=qmine.at[:, sent],
                    dst_ref=mine,
                    send_sem=send1,
                    recv_sem=recv1,
                    device_id={"seq": along_y(k)},
                    device_id_type=MESH,
                ).start()
            pltpu.make_async_copy(qmine.at[:, sent], mine, recv1).start()

    for load in loads:
        load.start()

    small[1].wait()
    small[2].wait()
    row16 = lax.broadcasted_iota(jnp.int32, (pages, LANES), 0)
    lane16 = lax.broadcasted_iota(jnp.int32, (pages, LANES), 1)
    own_row = jnp.zeros((pages, LANES), jnp.int32)
    own_lane = jnp.zeros((pages, LANES), jnp.int32)
    for p in range(pages):
        own_row = jnp.where(row16 == p, owner[p], own_row)
        own_lane = jnp.where((lane16 & (pages - 1)) == p, owner[p], own_lane)
    repeated = jnp.max(
        jnp.where((own_row == own_lane) & (row16 < (lane16 & (pages - 1))), 1, 0),
        axis=0, keepdims=True,
    )
    first_lane = jnp.where(repeated > 0, -1, own_lane[:1])
    big_row = lax.broadcasted_iota(jnp.int32, (seq * ROWS, LANES), 0)
    big_lane = lax.broadcasted_iota(jnp.int32, (seq * ROWS, LANES), 1)
    wanted = (first_lane * ROWS) + lax.div(big_lane[:1], pages)
    wanted = jnp.where((first_lane >= 0) & (big_lane[:1] < (heads + 1) * pages), wanted, -1)
    pick[...] = jnp.where(big_row == wanted, 1.0, 0.0).astype(jnp.bfloat16)
    own_rows = jnp.concatenate([own_row] * heads, axis=0)
    lane = lax.broadcasted_iota(jnp.int32, (1, LANES), 1)
    per = LANES // page
    for j in range(tokens // LANES):
        own_l = jnp.where(lane < page, owner[per * j], owner[per * j + 1])
        fill_l = jnp.where(lane < page, fill[per * j], fill[per * j + 1])
        own_l = jnp.where((lane & (page - 1)) < fill_l, own_l, -1)
        bias[:, j * LANES : (j + 1) * LANES] = jnp.where(own_rows == own_l, 0.0, EMPTY)

    def send_line(part, peers):
        mine = queries[part].at[pl.ds(block, ny), sent]
        for peer in peers:
            pltpu.make_async_remote_copy(
                src_ref=mine,
                dst_ref=mine,
                send_sem=send2,
                recv_sem=recv2.at[part],
                device_id={"seq": peer},
                device_id_type=MESH,
            ).start()

    for part, buf in enumerate(queries):

        @pl.when(late == part)
        def _(part=part, buf=buf):
            mine = buf.at[pl.ds(block, ny), sent]
            pltpu.make_async_copy(mine, mine, recv1).wait()
            if part == 0:
                for j in range(deep):
                    if j == deep - 1:
                        send_line(0, [like_core(0, k) for k in range(1, deep)])
                    pl.semaphore_wait(chip_in.at[j], 1)
                    send_line(0, [((deep + j) * ny + y) * 2 + core])
                for k in range(2 * deep):
                    tell(line_in.at[1], in_half(1, k))
            else:
                send_line(1, [like_core(0, k) for k in range(deep)])
                pl.semaphore_wait(line_in.at[1], 2 * deep)
                send_line(1, [like_core(1, k) for k in range(1, deep)])

    loads[1].wait()
    loads[2].wait()
    keys = cache[...].reshape(tokens, width)
    for h in range(heads):
        vproj[:, h * LANES : (h + 1) * LANES] = jnp.dot(
            keys[:, :latent], wuv[h], preferred_element_type=jnp.float32
        ).astype(jnp.bfloat16)

    swaps = []
    for part, buf in enumerate(queries):
        for own, lines in ((part, deep - 1), (1 - part, deep)):

            @pl.when(late == own)
            def _(part=part, buf=buf, lines=lines):
                rest = buf.at[pl.ds(0, lines * ny), sent]
                pltpu.make_async_copy(rest, rest, recv2.at[part]).wait()

        heard = buf.at[pl.ds(near, deep * ny), sent]
        swap = pltpu.make_async_remote_copy(
            src_ref=heard,
            dst_ref=heard,
            send_sem=send3.at[part],
            recv_sem=recv3.at[part],
            device_id={"seq": sibling},
            device_id_type=MESH,
        )
        swap.start()
        swaps.append(swap)
        swap.wait_recv()

        for p in range(pages):
            spot = owner[p] & (half - 1)
            at = ((spot & 1) * deep + spot // (2 * ny)) * ny + ((spot // 2) & (ny - 1))
            sel[p * ROWS : (p + 1) * ROWS, :] = buf[at].astype(jnp.float32)
        if part == 0:
            loads[0].wait()
        joined = []
        for h in range(heads):
            plain = sel[pl.ds(h, pages, stride=ROWS), :].astype(jnp.bfloat16)
            pair = sel[pl.ds(heads + h // 2, pages, stride=ROWS), :]
            turned = pair[:, (h % 2) * rope : (h % 2 + 1) * rope].astype(jnp.bfloat16)
            lat = jnp.dot(plain, wuk[h], preferred_element_type=jnp.float32)
            joined.append(jnp.concatenate([lat.astype(jnp.bfloat16), turned], axis=1))
        joined = jnp.concatenate(joined, axis=0)

        keys = cache[...].reshape(tokens, width)
        scores = lax.dot_general(
            joined, keys, (((1,), (1,)), ((), ())), preferred_element_type=jnp.float32
        )
        scores = scores * scale + bias[...]
        top = jnp.max(scores, axis=1, keepdims=True)
        top = jnp.where(top > 0.5 * EMPTY, top, 0.0)
        top_hi = top.astype(jnp.bfloat16).astype(jnp.float32)
        top_lo = (top - top_hi).astype(jnp.bfloat16).astype(jnp.float32)
        weights = jnp.exp(scores - (top_hi + top_lo))
        total = jnp.sum(weights, axis=1, keepdims=True)
        total_hi = total.astype(jnp.bfloat16).astype(jnp.float32)
        total_lo = total - total_hi
        sums = jnp.dot(
            weights.astype(jnp.bfloat16), vproj[...], preferred_element_type=jnp.float32
        )

        blocks = [
            sums[h * pages : (h + 1) * pages, h * LANES : (h + 1) * LANES] for h in range(heads)
        ]
        stats = jnp.zeros((pages, LANES), jnp.float32)
        for i, piece in enumerate((top_hi, top_lo, total_hi, total_lo)):
            for h in range(heads):
                stats = jnp.where(
                    lane16 == i * heads + h, piece[h * pages : (h + 1) * pages], stats
                )
        blocks += [stats, jnp.zeros((LANES - (heads + 1) * pages, LANES), jnp.float32)]
        table = jnp.concatenate(blocks, axis=0).astype(jnp.bfloat16)
        def send_sums(k, c, base):
            peer = base + k

            @pl.when(peer != me)
            def _():
                pltpu.make_async_remote_copy(
                    src_ref=sendb.at[peer, sent],
                    dst_ref=recvb.at[me, sent],
                    send_sem=bsend,
                    recv_sem=brecv,
                    device_id={"seq": peer},
                    device_id_type=MESH,
                ).start()

            return c

        for level in range(part * deep, (part + 1) * deep):
            many = 2 * ny
            sendb[pl.ds(level * many, many)] = (
                jnp.dot(
                    pick[pl.ds(level * many * ROWS, many * ROWS), :], table,
                    preferred_element_type=jnp.float32,
                )
                .astype(jnp.bfloat16)
                .reshape(many, ROWS, LANES)
            )
            lax.fori_loop(
                0, 2 * ny,
                functools.partial(send_sums, base=level * 2 * ny), 0,
            )

    recvb[me] = sendb[me]
    others = recvb.at[pl.ds(0, seq - 1), sent]
    pltpu.make_async_copy(others, others, brecv).wait()

    rf[...] = recvb[...].reshape(seq * ROWS, LANES).astype(jnp.float32)
    got = rf[pl.ds(heads, seq, stride=ROWS), :]
    tops = got + pltpu.roll(got, LANES - heads, 1)
    totals = pltpu.roll(got, LANES - 2 * heads, 1) + pltpu.roll(got, LANES - 3 * heads, 1)
    some = totals > 0.0
    tops = jnp.where(some, tops, EMPTY)
    peak = jnp.max(tops, axis=0, keepdims=True)
    share = jnp.where(some, jnp.exp(tops - peak), 0.0)
    denominator = jnp.sum(jnp.where(some, share * totals, 0.0), axis=0, keepdims=True)
    outs = []
    for h in range(heads):
        mine = rf[pl.ds(h, seq, stride=ROWS), :]
        numerator = jnp.sum(mine * share[:, h : h + 1], axis=0, keepdims=True)
        outs.append(numerator / denominator[:, h : h + 1])
    head_out = jnp.concatenate(outs, axis=1).astype(jnp.bfloat16)

    for load in loads[3:]:
        load.wait()
    sends = []
    for k in [2, 1, 3, 0]:
        peer = lax.rem(tx + k, tensor)
        piece = jnp.dot(head_out, wout[peer], preferred_element_type=jnp.float32)
        if k == 0:
            xr[tx] = piece
            continue
        xs[peer] = piece
        sends.append(
            pltpu.make_async_remote_copy(
                src_ref=xs.at[peer],
                dst_ref=xr.at[tx],
                send_sem=xsend.at[k],
                recv_sem=xrecv.at[k],
                device_id={"tensor": peer},
                device_id_type=MESH,
            )
        )
        sends[-1].start()
    for send in sends:
        send.wait_recv()
    total_value = xr[0]
    for t in range(1, tensor):
        total_value = total_value + xr[t]
    out_ref[...] = total_value.astype(out_ref.dtype)
    for send in sends:
        send.wait_send()
    away = qearly.at[pl.ds(0, ny - 1), sent]
    pltpu.make_async_copy(away, away, send1).wait()
    away = qearly.at[pl.ds(0, (nz - 1) * ny), sent]
    pltpu.make_async_copy(away, away, send2).wait()
    for swap in swaps:
        swap.wait_send()
    away = sendb.at[pl.ds(0, seq - 1), sent]
    pltpu.make_async_copy(away, away, bsend).wait()


def solution(mesh):
    seq, tensor = mesh.shape["seq"], mesh.shape["tensor"]

    def shards(query, page_owner, page_fill, cache, w_uk, w_uv, w_out):
        heads = w_uk.shape[0]
        width = query.shape[1] // heads
        columns = w_out.shape[1] // tensor
        ny = NY

        def body(*refs):
            kernel(seq, tensor, 1.0 / math.sqrt(width), ny, seq // (2 * ny), *refs)

        vmem = pl.BlockSpec(memory_space=pltpu.VMEM)
        hbm = pl.BlockSpec(memory_space=pltpu.HBM)
        dma = pltpu.SemaphoreType.DMA
        return pl.pallas_call(
            body,
            out_shape=pltpu.VMEM((query.shape[0], columns), jnp.bfloat16),
            in_specs=[hbm] * 7,
            out_specs=vmem,
            scratch_shapes=[
                pltpu.SMEM(page_owner.shape, page_owner.dtype),
                pltpu.SMEM(page_fill.shape, page_fill.dtype),
                pltpu.VMEM(query.shape, query.dtype),
                pltpu.VMEM((1, ROWS, LANES), jnp.bfloat16),
                pltpu.VMEM((seq // 2, ROWS, LANES), jnp.bfloat16),
                pltpu.VMEM((seq // 2, ROWS, LANES), jnp.bfloat16),
                pltpu.VMEM(cache.shape, cache.dtype),
                pltpu.VMEM(w_uk.shape, w_uk.dtype),
                pltpu.VMEM(w_uv.shape, w_uv.dtype),
                pltpu.VMEM((tensor, w_out.shape[0], columns), w_out.dtype),
                pltpu.VMEM((cache.shape[0] * cache.shape[1], heads * LANES), jnp.bfloat16),
                pltpu.VMEM((page_owner.shape[0] * heads, cache.shape[0] * cache.shape[1]), jnp.float32),
                pltpu.VMEM((page_owner.shape[0] * ROWS, LANES), jnp.float32),
                pltpu.VMEM((seq * ROWS, LANES), jnp.bfloat16),
                pltpu.VMEM((seq, ROWS, LANES), jnp.bfloat16),
                pltpu.VMEM((seq, ROWS, LANES), jnp.bfloat16),
                pltpu.VMEM((seq * ROWS, LANES), jnp.float32),
                pltpu.VMEM((tensor, 1, columns), jnp.float32),
                pltpu.VMEM((tensor, 1, columns), jnp.float32),
                pltpu.SemaphoreType.REGULAR((seq // (4 * ny),)),
                pltpu.SemaphoreType.REGULAR((2,)),
                dma((10,)),
                dma, dma, dma,
                dma((2,)),
                dma((2,)),
                dma((2,)),
                dma, dma,
                dma((tensor,)),
                dma((tensor,)),
            ],
            compiler_params=pltpu.CompilerParams(collective_id=0, has_side_effects=True),
        )(page_owner, page_fill, query, cache, w_uk, w_uv, w_out)

    return jax.shard_map(
        shards,
        mesh=mesh,
        in_specs=(
            P("seq", "tensor"), P("seq"), P("seq"), P("seq", None, None),
            P("tensor", None, None), P("tensor", None, None), P("tensor", None),
        ),
        out_specs=P("seq", "tensor"),
        check_vma=False,
    )
```
